32 devices in a mesh: section: 2 (over x), dp: 16 (over z, y, core).
Axes of the slice: x: 2, y: 2, z: 4, core: 2. Of those that a mesh axis runs over, the one named last changes fastest.
Arguments:
- section_rows: bfloat16 [2, 2048, 1024], P('section', 'dp'), may hold values from -6 to 6
- lang_ids: int32 [2048], P('dp'), may hold values from 0 to 199, as said below
- lang_table: int32 [200], replicated, may hold values from 0 to 7, as said below
- lang_counts: int32 [16, 200], P('dp'), may hold values from 4 to 210
- temp_num: int32 [200], replicated, may hold values from 1 to 16
- weights: bfloat16 [2, 1024, 32768], P('section', None, 'dp'), may hold values from -0.1875 to 0.1875
Outputs:
- grads: float32 [2, 1024, 32768], P('section', None, 'dp')
- input_grad: bfloat16 [2048, 1024], P('dp', 'section')
The draws below stay inside these ranges and needn't reach their ends.
Inputs may be any that keep to these rules, and one draw needn't show every extreme that they name: `lang_table`: every block is named by at least one language. `lang_ids`: on each replica (each aligned block of 128 rows) at most 32 rows map to any one block through lang_table, and one block receives exactly 32 rows from every replica.
All inputs are finite; a program needn't handle non-finite values.
Results may differ from the reference program's by a relative error of at most 0.0058.
Values may be sent and summed in bfloat16 or wider, within the bound.
No kernel may reach another device: no remote copies, remote signals or barrier semaphores. Data moves between devices by JAX's collectives and lax.ppermute only.
A program may use at most 64 MiB of HBM per device.

```python
import jax
import jax.numpy as jnp
from jax import lax

D = 1024
FF = 4096
LANGS = 200
ROWS_DEV = 128
REPLICAS = 16
BLOCKS = 8
CAP = 32
BLOCK_ROWS = 512
TOKENS = 2048


def block_order(key):
    return jax.random.permutation(jax.random.fold_in(key, 7), BLOCKS)


def draw_lang_table(key, part):
    order_table = block_order(key)
    return order_table[jnp.arange(LANGS) % BLOCKS].astype(jnp.int32)


def draw_lang_ids(key, part):
    base_key = jax.random.fold_in(key, 11)

    def one_replica(dev_key):
        key_slots, key_shuffle, key_lang = jax.random.split(dev_key, 3)
        band_first = BLOCKS // 4
        band_second = 5 * BLOCKS // 8
        slot_ids = jnp.arange((BLOCKS - 1) * CAP, dtype=jnp.int32)
        rank_of_slot = slot_ids // CAP + 1
        within = slot_ids % CAP
        avail = jnp.where(rank_of_slot < band_first, CAP, jnp.where(rank_of_slot < band_second, CAP // 2, CAP // 4))
        priority = jax.random.permutation(key_slots, (BLOCKS - 1) * CAP).astype(jnp.int32)
        priority = priority + jnp.where(within < avail, 0, (BLOCKS - 1) * CAP)
        chosen = jnp.argsort(priority)[:ROWS_DEV - CAP]
        ranks = jnp.concatenate([jnp.zeros((CAP,), jnp.int32), rank_of_slot[chosen]])
        ranks = jax.random.permutation(key_shuffle, ranks)
        options = (LANGS - ranks + BLOCKS - 1) // BLOCKS
        picked = jax.random.randint(key_lang, (ROWS_DEV,), 0, options)
        return (ranks + BLOCKS * picked).astype(jnp.int32)
    replica_keys = jax.random.split(base_key, REPLICAS)
    return jax.vmap(one_replica)(replica_keys).reshape(-1)


def draw_lang_counts(key, part):
    key_lang, key_jitter = jax.random.split(jax.random.fold_in(key, 13))
    lang_base = jax.random.randint(key_lang, (1, LANGS), 4, 64)
    jitter = jax.random.randint(key_jitter, (REPLICAS, LANGS), 0, 8)
    rising = REPLICAS - 1 + 2 * jnp.arange(REPLICAS, dtype=jnp.int32)[:, None]
    return ((lang_base + jitter) * rising // (REPLICAS - 1)).astype(jnp.int32)


def plant(values, key, low, top_value):
    extent = values.shape
    spot = [jax.random.randint(jax.random.fold_in(key, axis), (), 0, extent[axis]) for axis in range(len(extent))]
    values = values.at[tuple(spot)].set(low)
    longest = extent.index(max(extent))
    spot[longest] = (spot[longest] + 1) % extent[longest]
    return values.at[tuple(spot)].set(top_value)


def steps_of(own_key, dims, cuts, least, largest):
    loudness = 1.0
    for dim, parts in cuts:
        heights = jax.random.uniform(jax.random.fold_in(jax.random.fold_in(own_key, 6), dim), (parts,), jnp.float32, least / len(cuts), largest / len(cuts))
        loudness = loudness * jnp.repeat(jnp.exp(heights), dims[dim] // parts).reshape((-1,) + (1,) * (len(dims) - 1 - dim))
    return loudness


def normal_values(key, shape, scale, reach, pieces=(), held_as=jnp.bfloat16):
    values = scale * jax.random.normal(key, shape, jnp.float32)
    if pieces:
        values = values * steps_of(key, shape, pieces, -0.22, 0.18)
    return jnp.clip(values, -reach, reach).astype(held_as)


def setup_inputs(seed: int = 0) -> dict:
    key_of = jax.random.split(jax.random.key(seed), 7)
    section_rows = normal_values(key_of[0], (2, TOKENS, D), 1.0, 6.0, ((0, 2), (1, 16)))
    lang_ids = draw_lang_ids(jax.random.fold_in(key_of[6], 71), 0)
    lang_table = draw_lang_table(jax.random.fold_in(key_of[6], 71), 0)
    lang_counts = draw_lang_counts(jax.random.fold_in(key_of[6], 71), 0)
    temp_num = plant(jax.random.randint(key_of[4], (LANGS,), 1, 17), jax.random.fold_in(key_of[4], 1), 1, 16).astype(jnp.int32)
    weights = normal_values(key_of[5], (2, D, BLOCKS * FF), D ** -0.5, 0.1875, ((0, 2), (2, 16)))
    return dict(section_rows=section_rows, lang_ids=lang_ids, lang_table=lang_table, lang_counts=lang_counts, temp_num=temp_num, weights=weights)


def reference(section_rows, lang_ids, lang_table, lang_counts, temp_num, weights):
    token_count = section_rows.shape[1]
    row_block = lang_table[lang_ids]
    totals = jnp.sum(lang_counts.astype(jnp.float32), axis=0)
    lang_scale = 2.0 * REPLICAS * temp_num.astype(jnp.float32) / totals
    row_scale = lang_scale[lang_ids]
    padding = jnp.zeros((1, D), section_rows.dtype)
    layer_inputs = jnp.concatenate([section_rows[0], padding], axis=0)
    weighted = (section_rows[1] * row_scale[:, None]).astype(jnp.bfloat16)
    weighted = jnp.concatenate([weighted, padding.astype(jnp.bfloat16)], axis=0)
    up_all = weights[0].reshape(D, BLOCKS, FF)
    down_all = weights[1].reshape(D, BLOCKS, FF)
    contract_rows = (((0,), (0,)), ((), ()))

    def per_block(block_id):
        row_index = jnp.nonzero(row_block == block_id, size=BLOCK_ROWS, fill_value=token_count)[0].astype(jnp.int32)
        in_rows = layer_inputs[row_index]
        out_grads = weighted[row_index]
        up_cols = up_all[:, block_id, :]
        down_cols = down_all[:, block_id, :]
        pre_act = jnp.dot(in_rows, up_cols, preferred_element_type=jnp.float32)
        hidden = jnp.maximum(pre_act, 0.0).astype(jnp.bfloat16)
        down_grad = jnp.dot(out_grads, down_cols, preferred_element_type=jnp.float32).astype(jnp.bfloat16)
        up_grad = jnp.where(pre_act > 0.0, down_grad, jnp.zeros_like(down_grad))
        grad_up = lax.dot_general(in_rows, up_grad, contract_rows, preferred_element_type=jnp.float32)
        grad_down = lax.dot_general(out_grads, hidden, contract_rows, preferred_element_type=jnp.float32)
        row_grads = lax.dot_general(up_grad, up_cols, (((1,), (1,)), ((), ())), preferred_element_type=jnp.float32).astype(jnp.bfloat16)
        return grad_up, grad_down, row_grads, row_index

    grad_up, grad_down, row_grads, row_index = lax.map(per_block, jnp.arange(BLOCKS, dtype=jnp.int32))
    grads = jnp.stack([grad_up, grad_down]).transpose(0, 2, 1, 3).reshape(2, D, BLOCKS * FF)
    input_grad = jnp.zeros((token_count + 1, D), jnp.bfloat16).at[row_index.reshape(-1)].set(row_grads.reshape(-1, D))[:token_count]
    return grads, input_grad
```

```python
import jax
import jax.numpy as jnp
from jax import lax
from jax.sharding import PartitionSpec as P

HALVES = 2
PIECES = 2


def sibling(value):
    count = lax.axis_size("dp")
    return lax.ppermute(value, "dp", [(i, i ^ 1) for i in range(count)])


def across(value):
    return lax.ppermute(value, "section", [(0, 1), (1, 0)])


def same_core_exchange(value):
    count = lax.axis_size("dp")
    groups = [list(range(core, count, 2)) for core in range(2)]
    return lax.all_to_all(
        value, "dp", split_axis=0, concat_axis=0, axis_index_groups=groups, tiled=True
    )


def on_device(section_rows, lang_ids, lang_table, lang_counts, temp_num, weights):
    section_pos = lax.axis_index("section")
    is_up = section_pos == 0
    replicas = lax.axis_size("dp")
    blocks_all = replicas // 2
    rows_dev = lang_ids.shape[0]
    capacity = 2 * rows_dev // blocks_all
    half_cap = capacity // HALVES
    row_width = section_rows.shape[2]
    half_width = row_width // 2
    languages = lang_table.shape[0]
    own_weight = weights[0]
    local_rows = section_rows[0]

    lang_hot = lang_ids[:, None] == jnp.arange(languages, dtype=jnp.int32)[None, :]
    row_block = jnp.sum(jnp.where(lang_hot, lang_table[None, :], 0), axis=1)
    same = row_block[:, None] == row_block[None, :]
    earlier = jnp.arange(rows_dev)[None, :] < jnp.arange(rows_dev)[:, None]
    slot_index = jnp.sum((same & earlier).astype(jnp.int32), axis=1)
    target = (
        (slot_index // half_cap) * (blocks_all * half_cap)
        + row_block * half_cap
        + slot_index % half_cap
    )
    placing = target[None, :] == jnp.arange(blocks_all * capacity, dtype=jnp.int32)[:, None]
    place_hot = placing.astype(jnp.bfloat16)
    packed = jnp.dot(place_hot, local_rows, preferred_element_type=jnp.float32).astype(
        jnp.bfloat16
    )
    packed = packed.reshape(HALVES, blocks_all, half_cap, row_width)

    slot_lang = jnp.sum(jnp.where(placing, lang_ids[None, :], 0), axis=1)
    slot_lang = (
        slot_lang.reshape(HALVES, blocks_all, half_cap)
        .transpose(1, 0, 2)
        .reshape(blocks_all, capacity)
    )
    notes = jnp.concatenate(
        [jnp.broadcast_to(lang_counts, (blocks_all, languages)), slot_lang], axis=1
    )
    notes = jnp.repeat(notes, 2, axis=0)[:, None, :]
    notes = lax.all_to_all(notes, "dp", split_axis=0, concat_axis=0, tiled=True)[:, 0, :]
    totals = jnp.sum(notes[:, :languages].astype(jnp.float32), axis=0)
    lang_scale = 2.0 * replicas * temp_num.astype(jnp.float32) / totals
    core = lax.axis_index("dp") % 2
    came_lang = notes[:, languages:].reshape(blocks_all, 2, HALVES, half_cap)
    came_lang = jnp.where(core == 0, came_lang, came_lang[:, ::-1]).transpose(2, 1, 0, 3)
    came_hot = came_lang[..., None] == jnp.arange(languages, dtype=jnp.int32)
    came_scale = jnp.sum(jnp.where(came_hot, lang_scale, 0.0), axis=-1).reshape(HALVES, -1, 1)

    routed_parts, partner_parts, finals = [], [], []
    for half in range(HALVES):
        own = same_core_exchange(packed[half]).reshape(-1, row_width)
        other = sibling(own)
        routed = jnp.concatenate([own, other], axis=0)
        weighted = (routed * came_scale[half]).astype(jnp.bfloat16)
        routed = jnp.where(is_up, routed, weighted)
        routed_parts.append(routed)
        terms = []
        for piece in jnp.split(routed, PIECES, axis=0):
            projected = jnp.dot(piece, own_weight, preferred_element_type=jnp.float32)
            handed = jnp.where(is_up, jnp.maximum(projected, 0.0), projected).astype(jnp.bfloat16)
            received = across(handed)
            partner = jnp.where(is_up & (handed <= 0), jnp.zeros_like(received), received)
            partner_parts.append(partner)
            terms.append(
                lax.dot_general(
                    partner,
                    own_weight,
                    (((1,), (1,)), ((), ())),
                    preferred_element_type=jnp.float32,
                )
            )
        mine, theirs = terms
        summed = (mine + sibling(theirs)).astype(jnp.bfloat16)
        finals.append(same_core_exchange(summed.reshape(blocks_all, half_cap, row_width)))

    weight_grad = lax.dot_general(
        jnp.concatenate(routed_parts, axis=0),
        jnp.concatenate(partner_parts, axis=0),
        (((0,), (0,)), ((), ())),
        preferred_element_type=jnp.float32,
    )
    full_rows = lax.dot_general(
        place_hot,
        jnp.concatenate([f.reshape(-1, row_width) for f in finals], axis=0),
        (((0,), (0,)), ((), ())),
        preferred_element_type=jnp.float32,
    ).astype(jnp.bfloat16)
    right_cols = lax.ppermute(full_rows[:, half_width:], "section", [(0, 1)])
    input_grad = jnp.where(is_up, full_rows[:, :half_width], right_cols)
    return (weight_grad[None], input_grad)


def solution(mesh):
    return jax.shard_map(
        on_device,
        mesh=mesh,
        in_specs=(
            P("section", "dp", None),
            P("dp"),
            P(),
            P("dp", None),
            P(),
            P("section", None, "dp"),
        ),
        out_specs=(P("section", None, "dp"), P("dp", "section")),
        check_vma=False,
    )
```

```python
import jax
import jax.numpy as jnp
from jax import lax
from jax.sharding import PartitionSpec as P

F32 = jnp.float32
BF16 = jnp.bfloat16


def sibling(value):
    count = lax.axis_size("dp")
    return lax.ppermute(value, "dp", [(i, i ^ 1) for i in range(count)])


def relation(value, rel):
    count = lax.axis_size("dp")
    return lax.ppermute(value, "dp", [(i, i ^ (2 * rel)) for i in range(count)])


def across(value):
    return lax.ppermute(value, "section", [(0, 1), (1, 0)])


def same_core_exchange(value):
    count = lax.axis_size("dp")
    groups = [list(range(core, count, 2)) for core in range(2)]
    return lax.all_to_all(
        value, "dp", split_axis=0, concat_axis=0, axis_index_groups=groups, tiled=True
    )


def chip_piece(stack, chip):
    return lax.dynamic_index_in_dim(stack, chip, axis=0, keepdims=False)


def on_device(section_rows, lang_ids, lang_table, lang_counts, temp_num, weights):
    is_up = lax.axis_index("section") == 0
    replicas = lax.axis_size("dp")
    place_index = lax.axis_index("dp")
    chip = place_index // 2
    core = place_index % 2
    chips = replicas // 2
    unit = chips // 8
    rows_dev = lang_ids.shape[0]
    capacity = 2 * rows_dev // chips
    row_width = section_rows.shape[2]
    half_width = row_width // 2
    languages = lang_table.shape[0]
    own_weight = weights[0]
    local_rows = section_rows[0]

    lang_hot = lang_ids[:, None] == jnp.arange(languages, dtype=jnp.int32)[None, :]
    row_block = jnp.sum(jnp.where(lang_hot, lang_table[None, :], 0), axis=1)
    same = row_block[:, None] == row_block[None, :]
    earlier = jnp.arange(rows_dev)[None, :] < jnp.arange(rows_dev)[:, None]
    slot_index = jnp.sum((same & earlier).astype(jnp.int32), axis=1)
    target = row_block * capacity + slot_index
    row_rel = row_block ^ chip
    near_target = row_rel * capacity + slot_index
    placing = target[None, :] == jnp.arange(chips * capacity, dtype=jnp.int32)[:, None]
    place_hot = placing.astype(BF16)
    packed = jnp.dot(place_hot, local_rows, preferred_element_type=F32).astype(BF16)
    packed = packed.reshape(chips, capacity, row_width)
    near_rows = jnp.concatenate([chip_piece(packed, chip ^ r) for r in range(2 * unit)], axis=0)

    came = same_core_exchange(packed)
    near_other = sibling(near_rows)
    size0 = unit * capacity
    rows_own = jnp.concatenate([near_rows[:size0], near_other[:size0]], axis=0)
    rows_next = jnp.concatenate([near_rows[size0:], near_other[size0:]], axis=0)
    if unit == 1:
        rows_next = relation(rows_next, 1)
    else:
        shaped = rows_next.reshape(2 * unit, capacity, row_width)
        rows_own_list = rows_own.reshape(2 * unit, capacity, row_width)
        moved = [
            relation(jnp.stack([rows_own_list[r], rows_own_list[unit + r]]), r)
            for r in range(1, unit)
        ]
        moved = [jnp.stack([rows_own_list[0], rows_own_list[unit]])] + moved
        rows_own = jnp.stack(moved, axis=1).reshape(-1, row_width)
        moved = [
            relation(jnp.stack([shaped[r], shaped[unit + r]]), unit + r) for r in range(unit)
        ]
        rows_next = jnp.stack(moved, axis=1).reshape(-1, row_width)

    def rels(first, last):
        return list(range(first * unit, last * unit))

    far_groups = [rels(4, 6), rels(6, 8), rels(2, 4)]
    far_own = jnp.concatenate(
        [chip_piece(came, chip ^ r) for group in far_groups for r in group], axis=0
    )
    far_other = sibling(far_own)
    groups = [rels(0, 1), rels(1, 2)] + far_groups
    group_rows = [rows_own, rows_next]
    size = 2 * unit * capacity
    for i in range(len(far_groups)):
        group_rows.append(
            jnp.concatenate(
                [far_own[i * size : (i + 1) * size], far_other[i * size : (i + 1) * size]], axis=0
            )
        )

    slot_lang = jnp.sum(jnp.where(placing, lang_ids[None, :], 0), axis=1)
    slot_lang = slot_lang.reshape(chips, capacity)
    notes = jnp.concatenate(
        [jnp.broadcast_to(lang_counts, (chips, languages)), slot_lang], axis=1
    )
    notes = jnp.repeat(notes, 2, axis=0)[:, None, :]

    handed, received = [], []
    for i, rows in enumerate(group_rows):
        projected = jnp.dot(rows, own_weight, preferred_element_type=F32)
        hand = jnp.where(is_up, jnp.maximum(projected, 0.0), projected).astype(BF16)
        handed.append(hand)
        received.append(across(hand))
        if i == 2:
            notes, _ = lax.optimization_barrier((notes, hand))

    notes = lax.all_to_all(notes, "dp", split_axis=0, concat_axis=0, tiled=True)[:, 0, :]
    totals = jnp.sum(notes[:, :languages].astype(F32), axis=0)
    lang_scale = 2.0 * replicas * temp_num.astype(F32) / totals
    came_lang = notes[:, languages:].reshape(chips, 2, capacity)
    came_lang = jnp.where(core == 0, came_lang, came_lang[:, ::-1])
    came_hot = came_lang[..., None] == jnp.arange(languages, dtype=jnp.int32)
    came_scale = jnp.sum(jnp.where(came_hot, lang_scale, 0.0), axis=-1)
    rel_scale = [chip_piece(came_scale, chip ^ r) for r in range(chips)]

    direct = rels(0, 1) + rels(2, 4)
    scaled_rows, partners, sums = [], [], {}
    for i, (group, rows, hand, recv) in enumerate(zip(groups, group_rows, handed, received)):
        if i < 2:
            recv, _ = lax.optimization_barrier((recv, handed[-1]))
        if i == len(groups) - 1:
            stack = jnp.stack([sums[r] if r not in direct else sums[unit] for r in range(chips)])
            stack = jnp.stack([chip_piece(stack, chip ^ j) for j in range(chips)])
            recv, stack = lax.optimization_barrier((recv, stack))
        partner = jnp.where(is_up & (hand <= 0), jnp.zeros_like(recv), recv)
        partners.append(partner)
        count = rows.shape[0] // 2
        terms = [
            lax.dot_general(
                part, own_weight, (((1,), (1,)), ((), ())), preferred_element_type=F32
            )
            for part in (partner[:count], partner[count:])
        ]
        scale = jnp.stack([rel_scale[r] for r in group], axis=1).reshape(-1, 1)
        scaled_rows.append((rows * scale).astype(BF16))
        summed = ((terms[0] + sibling(terms[1])) * scale[:count]).astype(BF16)
        for j, r in enumerate(group):
            sums[r] = summed[j * capacity : (j + 1) * capacity]

    back = same_core_exchange(stack)
    final = [back.reshape(-1, row_width)]
    far_hot = jnp.where((row_rel >= 2 * unit) & (row_rel < 4 * unit), -1, target)
    far_hot = jnp.where(row_rel < unit, -1, far_hot)
    hots = [
        (far_hot[None, :] == jnp.arange(chips * capacity, dtype=jnp.int32)[:, None]).astype(BF16)
    ]
    for r in direct:
        final.append(relation(sums[r], r) if r else sums[r])
        hots.append(
            (
                near_target[None, :]
                == (r * capacity + jnp.arange(capacity, dtype=jnp.int32))[:, None]
            ).astype(BF16)
        )
    weight_grad = lax.dot_general(
        jnp.concatenate(scaled_rows, axis=0),
        jnp.concatenate(partners, axis=0),
        (((0,), (0,)), ((), ())),
        preferred_element_type=F32,
    )
    full_rows = lax.dot_general(
        jnp.concatenate(hots, axis=0),
        jnp.concatenate(final, axis=0),
        (((0,), (0,)), ((), ())),
        preferred_element_type=F32,
    ).astype(BF16)
    right_cols = lax.ppermute(full_rows[:, half_width:], "section", [(0, 1)])
    input_grad = jnp.where(is_up, full_rows[:, :half_width], right_cols)
    return (weight_grad[None], input_grad)


def solution(mesh):
    return jax.shard_map(
        on_device,
        mesh=mesh,
        in_specs=(
            P("section", "dp", None),
            P("dp"),
            P(),
            P("dp", None),
            P(),
            P("section", None, "dp"),
        ),
        out_specs=(P("section", None, "dp"), P("dp", "section")),
        check_vma=False,
    )
```

```python
import functools

import jax
import jax.numpy as jnp
from jax import lax
from jax.experimental import pallas as pl
from jax.experimental.pallas import tpu as pltpu
from jax.sharding import PartitionSpec as P

F32 = jnp.float32
BF16 = jnp.bfloat16
I32 = jnp.int32
LANG_LANE = 256
VMEM = pl.BlockSpec(memory_space=pltpu.VMEM)


def sds(shape, dtype):
    return jax.ShapeDtypeStruct(shape, dtype)


def call(kernel, outs, *args, scratch=(), limit=8, spec=VMEM):
    return pl.pallas_call(
        kernel,
        out_shape=outs,
        in_specs=[spec] * len(args),
        out_specs=jax.tree.map(lambda _: VMEM, outs),
        scratch_shapes=list(scratch),
        compiler_params=pltpu.CompilerParams(vmem_limit_bytes=limit << 20),
        cost_estimate=pl.CostEstimate(flops=1000, bytes_accessed=1000, transcendentals=0),
    )(*args)


def sibling(value):
    count = lax.axis_size("dp")
    return lax.ppermute(value, "dp", [(i, i ^ 1) for i in range(count)])


def relation(value, rel):
    if rel == 0:
        return value
    count = lax.axis_size("dp")
    return lax.ppermute(value, "dp", [(i, i ^ (2 * rel)) for i in range(count)])


def across(values):
    return tuple(lax.ppermute(value, "section", [(0, 1), (1, 0)]) for value in values)


def same_core_exchange(value):
    count = lax.axis_size("dp")
    groups = [list(range(core, count, 2)) for core in range(2)]
    return lax.all_to_all(
        value, "dp", split_axis=0, concat_axis=0, axis_index_groups=groups, tiled=True
    )


def after(value, *others):
    return lax.optimization_barrier((value, *others))[0]


def pieces_of(count, cap):
    return [(i, core * cap) for core in range(2) for i in range(count)]


def iota(shape, dim):
    return lax.broadcasted_iota(I32, shape, dim)


def place_kernel(near_rels, *refs):
    inputs, (packed, near, info, notes), copies = refs[:4], refs[4:8], refs[8:]
    moves = [
        pltpu.make_async_copy(src, dst, copies[4].at[i])
        for i, (src, dst) in enumerate(zip(inputs, copies))
    ]
    for move in moves:
        move.start()
    for move in moves:
        move.wait()
    ids, table, counts, rows = copies[:4]
    chips, cap, _ = packed.shape
    chip = lax.axis_index("dp") // 2
    rows_dev = ids.shape[1]
    languages = table.shape[1]
    lang = ids[...]
    lang_hot = (iota((languages, rows_dev), 0) == lang).astype(F32)
    block = jnp.dot(table[...].astype(F32), lang_hot, preferred_element_type=F32).astype(I32)
    block_hot = iota((chips, rows_dev), 0) == block
    earlier = (iota((rows_dev, rows_dev), 0) < iota((rows_dev, rows_dev), 1)).astype(BF16)
    running = jnp.dot(
        block_hot.astype(F32).astype(BF16), earlier, preferred_element_type=F32
    )
    slot = jnp.sum(jnp.where(block_hot, running, 0.0), axis=0, keepdims=True).astype(I32)
    target = block * cap + slot
    hot = (iota((chips * cap, rows_dev), 0) == target).astype(F32).astype(BF16)
    values = rows[...]
    packed[...] = (
        jnp.dot(hot, values, preferred_element_type=F32).astype(BF16).reshape(packed.shape)
    )
    near_target = jnp.full_like(target, -1)
    for place, rel in enumerate(near_rels):
        near_target = jnp.where((block ^ chip) == rel, place * cap + slot, near_target)
    hot = (iota((len(near_rels) * cap, rows_dev), 0) == near_target).astype(F32).astype(BF16)
    near[...] = jnp.dot(hot, values, preferred_element_type=F32).astype(BF16)
    info[0:1, :] = block ^ chip
    info[1:2, :] = slot
    info[2:, :] = jnp.zeros((info.shape[0] - 2, rows_dev), I32)
    block_hot = (iota((2 * chips, rows_dev), 0) // 2 == block).astype(F32)
    slot_hot = (iota((cap, rows_dev), 0) == slot).astype(F32).astype(BF16)
    slot_lang = lax.dot_general(
        (block_hot * lang.astype(F32)).astype(BF16),
        slot_hot,
        (((1,), (1,)), ((), ())),
        preferred_element_type=F32,
    )
    notes[...] = jnp.zeros_like(notes)
    notes[:, :languages] = jnp.broadcast_to(counts[...], (2 * chips, languages))
    notes[:, LANG_LANE : LANG_LANE + cap] = slot_lang.astype(I32)


def packets_kernel(own, other, *outs):
    half = outs[0].shape[0] // 2
    for i, out in enumerate(outs):
        out[:half] = own[i * half : (i + 1) * half]
        out[half:] = other[i * half : (i + 1) * half]


def gather_kernel(rels, stack, out):
    chip = lax.axis_index("dp") // 2
    cap = stack.shape[1]
    for i, rel in enumerate(rels):
        out[i * cap : (i + 1) * cap, :] = stack[chip ^ rel]


def tail_kernel(layout, cap, notes, temp, *refs):
    inputs, scale_out, turned, langs, lhs = refs[:-4], refs[-4], refs[-3], refs[-2], refs[-1]
    device = lax.axis_index("dp")
    languages = temp.shape[1]
    totals = jnp.sum(notes[...].astype(F32), axis=0)[:, :languages]
    lang_scale = 2.0 * notes.shape[0] * temp[...].astype(F32) / totals
    for i, (rel, core, _, _) in enumerate(layout):
        source = device ^ (2 * rel + core)
        langs[i : i + 1, :] = notes[source, :, LANG_LANE : LANG_LANE + 128]
    lang_columns = langs[...].T
    for i, (_, _, which, first) in enumerate(layout):
        column = lang_columns[:cap, i : i + 1]
        scale = jnp.sum(
            jnp.where(column == iota((cap, languages), 1), lang_scale, 0.0),
            axis=1,
            keepdims=True,
        )
        scale_out[i * cap : (i + 1) * cap, :] = scale
        rows = inputs[which][first : first + cap, :].astype(F32) * scale
        lhs[i * cap : (i + 1) * cap, :] = rows.astype(BF16)
    turned[...] = lhs[...].T


def product_kernel(count, pieces, *refs):
    inputs, weight, hands, rows = refs[:count], refs[count], refs[count + 1 : -1], refs[-1]
    cap = rows.shape[0] // len(pieces)
    is_up = lax.axis_index("section") == 0
    for i, (which, first) in enumerate(pieces):
        rows[i * cap : (i + 1) * cap, :] = inputs[which][first : first + cap, :]
    tile = 512
    for j in range(0, weight.shape[1], tile):
        value = jnp.dot(rows[...], weight[:, j : j + tile], preferred_element_type=F32)
        value = jnp.where(is_up, jnp.maximum(value, 0.0), value).astype(BF16)
        first = 0
        for hand in hands:
            hand[:, j : j + tile] = value[first : first + hand.shape[0]]
            first += hand.shape[0]


def join_kernel(cap, first, mine, theirs, scale, *outs):
    for j, out in enumerate(outs):
        rows = slice(j * cap, (j + 1) * cap)
        factor = scale[first + j * cap : first + (j + 1) * cap, :]
        out[...] = ((mine[rows, :] + theirs[rows, :]) * factor).astype(BF16)


def back_kernel(*refs):
    count = (len(refs) - 4) // 2
    recvs, hands, (weight, partner, mine, theirs) = refs[:count], refs[count:-4], refs[-4:]
    is_up = lax.axis_index("section") == 0
    half = mine.shape[0]
    masked = is_up & (jnp.concatenate([h[...] for h in hands], axis=0) <= 0)
    recv = jnp.concatenate([r[...] for r in recvs], axis=0)
    value = jnp.where(masked, jnp.zeros_like(recv), recv)
    partner[...] = value
    product = lax.dot_general(
        value, weight[...], (((1,), (1,)), ((), ())), preferred_element_type=F32
    )
    mine[...] = product[:half]
    theirs[...] = product[half:]


def weight_kernel(turned, *refs):
    partners, out = refs[:-1], refs[-1]
    rhs = jnp.concatenate([p[...] for p in partners], axis=0)
    out[...] = jnp.dot(turned[...], rhs, preferred_element_type=F32)


def final_kernel(direct, cap, info, *refs):
    pieces, left, right = refs[:-2], refs[-2], refs[-1]
    rel, slot = info[0:1, :], info[1:2, :]
    rows_dev = rel.shape[1]
    target = jnp.zeros_like(rel)
    for i, r in enumerate(direct):
        target = jnp.where(rel == r, i * cap + slot, target)
    values = jnp.concatenate([p[...] for p in pieces], axis=0)
    hot = (iota((values.shape[0], rows_dev), 0) == target).astype(F32).astype(BF16)
    rows = lax.dot_general(
        hot, values, (((0,), (0,)), ((), ())), preferred_element_type=F32
    ).astype(BF16)
    half = left.shape[1]
    left[...] = rows[:, :half]
    right[...] = rows[:, half:]


def on_device(section_rows, lang_ids, lang_table, lang_counts, temp_num, weights):
    is_up = lax.axis_index("section") == 0
    replicas = lax.axis_size("dp")
    chips = replicas // 2
    unit = chips // 8
    rows_dev = lang_ids.shape[0]
    cap = 2 * rows_dev // chips
    width = section_rows.shape[2]
    own_weight = weights[0]
    ff_dev = own_weight.shape[1]

    def rels(first, last):
        return list(range(first * unit, last * unit))

    groups = [rels(0, 1), rels(2, 4), rels(4, 6), rels(6, 8), rels(1, 2)]
    near_rels = groups[0] + groups[1]
    far_rels = groups[2] + groups[3] + groups[4]
    table = lang_table.reshape(1, -1)

    packed, near, info, notes = call(
        functools.partial(place_kernel, near_rels),
        (
            sds((chips, cap, width), BF16),
            sds((len(near_rels) * cap, width), BF16),
            sds((8, rows_dev), I32),
            sds((2 * chips, LANG_LANE + 128), I32),
        ),
        lang_ids.reshape(1, -1),
        table,
        lang_counts,
        section_rows[0],
        scratch=[
            pltpu.VMEM((1, rows_dev), I32),
            pltpu.VMEM(table.shape, I32),
            pltpu.VMEM(lang_counts.shape, I32),
            pltpu.VMEM((rows_dev, width), BF16),
            pltpu.SemaphoreType.DMA((4,)),
        ],
        spec=pl.BlockSpec(memory_space=pl.ANY),
    )
    came = same_core_exchange(packed)
    near_other = sibling(near)
    packets = call(
        packets_kernel,
        tuple(sds((2 * cap, width), BF16) for _ in near_rels),
        near,
        near_other,
    )
    moved = {r: relation(p, r) for r, p in zip(near_rels, packets)}

    hands, received, partners, terms = [], [], [], []

    def product(inputs, pieces, parts=1):
        count = len(pieces) * cap
        hand = call(
            functools.partial(product_kernel, len(inputs), pieces),
            (sds((count // parts, ff_dev), BF16),) * parts,
            *inputs,
            own_weight,
            scratch=[pltpu.VMEM((count, width), BF16)],
        )
        hands.append(hand)
        received.append(across(hand))

    def back_product(g, *earlier):
        count = len(groups[g]) * cap
        partner, mine, theirs = call(
            back_kernel,
            (sds((2 * count, ff_dev), BF16), sds((count, width), F32), sds((count, width), F32)),
            *lax.optimization_barrier((*received[g], *earlier))[: len(received[g])],
            *hands[g],
            own_weight,
        )
        partners.append(partner)
        terms.append((mine, sibling(theirs)))

    product([moved[r] for r in groups[0]], pieces_of(len(groups[0]), cap))
    inputs = [moved[r] for r in groups[1]]
    inputs[0] = after(inputs[0], *hands[0])
    product(inputs, pieces_of(len(groups[1]), cap), parts=2)
    came = after(came, *received[0], received[1][0])
    far_own = call(
        functools.partial(gather_kernel, far_rels),
        sds((len(far_rels) * cap, width), BF16),
        came,
    )
    far_other = sibling(far_own)
    far_pieces, start = [], 0
    for g in range(2, 5):
        size = len(groups[g])
        far_pieces.append([(c, (start + i) * cap) for c in range(2) for i in range(size)])
        start += size
    product([far_own, far_other], far_pieces[0])
    product([after(far_own, *received[1], *hands[2]), far_other], far_pieces[1])

    notes = after(notes, *hands[3])
    notes = lax.all_to_all(
        notes.reshape(2 * chips, 1, -1), "dp", split_axis=0, concat_axis=0, tiled=True
    )
    back_product(0, *hands[3])
    back_product(1, partners[0])

    inputs = [moved[r] for r in near_rels] + [far_own, far_other]
    layout, group_first = [], []
    for g, group in enumerate(groups):
        group_first.append(len(layout) * cap)
        for core in range(2):
            for r in group:
                if g < 2:
                    layout.append((r, core, near_rels.index(r), core * cap))
                else:
                    layout.append((r, core, len(near_rels) + core, far_rels.index(r) * cap))
    total_rows = len(layout) * cap
    scale, turned = call(
        functools.partial(tail_kernel, layout, cap),
        (sds((total_rows, 1), F32), sds((width, total_rows), BF16)),
        notes,
        temp_num.reshape(1, -1),
        *inputs,
        scratch=[
            pltpu.VMEM((max(len(layout), 8), 128), I32),
            pltpu.VMEM((total_rows, width), BF16),
        ],
    )
    returned = {}

    def give_back(g):
        joined = call(
            functools.partial(join_kernel, cap, group_first[g]),
            tuple(sds((cap, width), BF16) for _ in groups[g]),
            *terms[g],
            scale,
        )
        for rows, r in zip(joined, groups[g]):
            returned[r] = relation(rows, r)

    def given(g):
        return [returned[r] for r in groups[g]]

    give_back(0)
    give_back(1)
    product([after(far_own, *received[2], scale), far_other], far_pieces[2])
    back_product(2, *hands[4])
    give_back(2)
    back_product(3, partners[2], *given(1))
    give_back(3)
    back_product(4, partners[3], *given(2))
    give_back(4)
    direct = [r for group in groups for r in group]
    left, right = call(
        functools.partial(final_kernel, direct, cap),
        (sds((rows_dev, width // 2), BF16),) * 2,
        info,
        *[returned[r] for r in direct],
    )
    right_cols = lax.ppermute(right, "section", [(0, 1)])
    input_grad = jnp.where(is_up, left, right_cols)
    tile = 256
    weight_grad = pl.pallas_call(
        weight_kernel,
        out_shape=sds((width, ff_dev), F32),
        grid=(ff_dev // tile,),
        in_specs=[pl.BlockSpec((width, total_rows), lambda j: (0, 0))]
        + [pl.BlockSpec((p.shape[0], tile), lambda j: (0, j)) for p in partners],
        out_specs=pl.BlockSpec((width, tile), lambda j: (0, j)),
        compiler_params=pltpu.CompilerParams(vmem_limit_bytes=12 << 20),
        cost_estimate=pl.CostEstimate(
            flops=2 * width * total_rows * ff_dev,
            bytes_accessed=4 * width * ff_dev,
            transcendentals=0,
        ),
    )(turned, *partners)
    return (weight_grad[None], input_grad)


def solution(mesh):
    return jax.shard_map(
        on_device,
        mesh=mesh,
        in_specs=(
            P("section", "dp", None),
            P("dp"),
            P(),
            P("dp", None),
            P(),
            P("section", None, "dp"),
        ),
        out_specs=(P("section", None, "dp"), P("dp", "section")),
        check_vma=False,
    )
```

```python
import functools

import jax
import jax.numpy as jnp
from jax import lax
from jax.experimental import pallas as pl
from jax.experimental.pallas import tpu as pltpu
from jax.sharding import PartitionSpec as P

F32 = jnp.float32
BF16 = jnp.bfloat16
I32 = jnp.int32
NOTES = 128
VMEM = pl.BlockSpec(memory_space=pltpu.VMEM)


def sds(shape, dtype):
    return jax.ShapeDtypeStruct(shape, dtype)


def call(kernel, outs, *args, scratch=(), limit=8, spec=VMEM):
    return pl.pallas_call(
        kernel,
        out_shape=outs,
        in_specs=[spec] * len(args),
        out_specs=jax.tree.map(lambda _: VMEM, outs),
        scratch_shapes=list(scratch),
        compiler_params=pltpu.CompilerParams(vmem_limit_bytes=limit << 20),
        cost_estimate=pl.CostEstimate(flops=1000, bytes_accessed=1000, transcendentals=0),
    )(*args)


def sibling(value):
    count = lax.axis_size("dp")
    return lax.ppermute(value, "dp", [(i, i ^ 1) for i in range(count)])


def across(values):
    return tuple(lax.ppermute(value, "section", [(0, 1), (1, 0)]) for value in values)


def same_core_exchange(value):
    count = lax.axis_size("dp")
    groups = [list(range(core, count, 2)) for core in range(2)]
    return lax.all_to_all(
        value, "dp", split_axis=0, concat_axis=0, axis_index_groups=groups, tiled=True
    )


def after(value, *others):
    return lax.optimization_barrier((value, *others))[0]


def iota(shape, dim):
    return lax.broadcasted_iota(I32, shape, dim)


def place_kernel(*refs):
    inputs, (*packed, info), copies = refs[:4], refs[4:-5], refs[-5:]
    moves = [
        pltpu.make_async_copy(src, dst, copies[4].at[i])
        for i, (src, dst) in enumerate(zip(inputs, copies))
    ]
    for move in moves:
        move.start()
    for move in moves:
        move.wait()
    ids, table, counts, rows = copies[:4]
    chips, part, _ = packed[0].shape
    width = rows.shape[1]
    chip = lax.axis_index("dp") // 2
    rows_dev = ids.shape[1]
    languages = table.shape[1]
    lang = ids[...]
    lang_hot = (iota((languages, rows_dev), 0) == lang).astype(F32)
    block = jnp.dot(table[...].astype(F32), lang_hot, preferred_element_type=F32).astype(I32)
    block_hot = iota((chips, rows_dev), 0) == block
    earlier = (iota((rows_dev, rows_dev), 0) < iota((rows_dev, rows_dev), 1)).astype(BF16)
    running = jnp.dot(
        block_hot.astype(F32).astype(BF16), earlier, preferred_element_type=F32
    )
    slot = jnp.sum(jnp.where(block_hot, running, 0.0), axis=0, keepdims=True).astype(I32)
    info[0:1, :] = slot
    info[1:2, :] = block
    info[2:, :] = jnp.zeros((info.shape[0] - 2, rows_dev), I32)
    values = counts[...].astype(F32)
    blank = jnp.zeros((1, 2 * NOTES - 2 - languages), F32)
    tail = jnp.concatenate([values[:, NOTES - 1 :], blank, jnp.zeros((1, 1), F32)], axis=1)
    head = jnp.concatenate([values[:, : NOTES - 1], jnp.zeros((1, 1), F32)], axis=1)

    def slots(target, count, first):
        hot = iota((count, rows_dev), 0) == target
        moved = jnp.dot(
            hot.astype(F32).astype(BF16), rows[...], preferred_element_type=F32
        ).astype(BF16)
        slot_lang = jnp.sum(jnp.where(hot, lang, 0), axis=1, keepdims=True).astype(F32)
        notes = jnp.where(iota((count, NOTES), 1) == NOTES - 1, slot_lang, 0.0)
        if first:
            within = iota((count, NOTES), 0) % part
            notes = notes + jnp.where(within == 0, head, 0.0) + jnp.where(within == 1, tail, 0.0)
        return moved, notes.astype(BF16)

    for p, out in enumerate(packed):
        inside = (slot // part) == p
        target = jnp.where(inside, block * part + slot % part, -1)
        moved, notes = slots(target, chips * part, p == 0)
        out[:, :, :width] = moved.reshape(chips, part, width)
        out[:, :, width:] = notes.reshape(chips, part, NOTES)


def load_piece(inputs, piece):
    which, first, rel, size = piece
    if rel is None:
        return inputs[which][first : first + size, :]
    return inputs[which][(lax.axis_index("dp") // 2) ^ rel]


def tail_kernel(pieces, sources, temp, *refs):
    inputs, scale_out, turned, lhs = refs[:-3], refs[-3], refs[-2], refs[-1]
    width, languages = lhs.shape[1], temp.shape[1]
    totals = [0.0, 0.0]
    for source in sources:
        for row in range(2):
            for c in range(inputs[source].shape[0]):
                totals[row] = totals[row] + inputs[source][c, row : row + 1, width:].astype(F32)
    values = temp[...].astype(F32)
    blank = jnp.zeros((1, 2 * NOTES - 2 - languages), F32)
    pads = jnp.zeros((1, 1), F32)
    numer = [
        jnp.concatenate([values[:, : NOTES - 1], pads], axis=1),
        jnp.concatenate([values[:, NOTES - 1 :], blank, pads], axis=1),
    ]
    factor = 2.0 * lax.axis_size("dp")
    lane = iota((1, NOTES), 1)
    valid = [lane < NOTES - 1, lane < languages - (NOTES - 1)]
    table = [
        jnp.where(ok, factor * n / jnp.where(ok, t, 1.0), 0.0)
        for n, t, ok in zip(numer, totals, valid)
    ]
    first = 0
    for piece in pieces:
        size = piece[3]
        values = load_piece(inputs, piece).astype(F32)
        lang = values[:, width + NOTES - 1 :].astype(I32)
        number = iota((size, NOTES), 1)
        hit = jnp.where(lang == number, table[0], 0.0) + jnp.where(
            lang - (NOTES - 1) == number, table[1], 0.0
        )
        scale = jnp.sum(hit, axis=1, keepdims=True)
        scale_out[first : first + size, :] = scale
        lhs[first : first + size, :] = (values[:, :width] * scale).astype(BF16)
        first += size
    turned[...] = lhs[...].T


def product_kernel(count, pieces, *refs):
    inputs, weight, hands, rows = refs[:count], refs[count], refs[count + 1 : -1], refs[-1]
    width = rows.shape[1]
    is_up = lax.axis_index("section") == 0
    first = 0
    for piece in pieces:
        size = piece[3]
        rows[first : first + size, :] = load_piece(inputs, piece)[:, :width]
        first += size
    tile = 512
    for j in range(0, weight.shape[1], tile):
        value = jnp.dot(rows[...], weight[:, j : j + tile], preferred_element_type=F32)
        value = jnp.where(is_up, jnp.maximum(value, 0.0), value).astype(BF16)
        first = 0
        for hand in hands:
            hand[:, j : j + tile] = value[first : first + hand.shape[0]]
            first += hand.shape[0]


def stack_kernel(first, count, scale, *rest):
    mine, theirs, out = rest[:count], rest[count:-1], rest[-1]
    chip = lax.axis_index("dp") // 2
    chips, part, _ = out.shape
    total = jnp.concatenate([m[...] for m in mine], axis=0)
    total = total + jnp.concatenate([t[...] for t in theirs], axis=1)
    total = (total * scale[first : first + part * chips, :]).astype(BF16)
    for rel in range(chips):
        out[chip ^ rel] = total[rel * part : (rel + 1) * part]


def back_kernel(recv, hand, weight, partner, *outs):
    is_up = lax.axis_index("section") == 0
    masked = is_up & (hand[...] <= 0)
    value = jnp.where(masked, jnp.zeros_like(recv), recv[...])
    partner[...] = value
    product = lax.dot_general(
        value, weight[...], (((1,), (1,)), ((), ())), preferred_element_type=F32
    )
    first = 0
    column = 0
    for out in outs:
        size, columns = out.shape
        out[...] = product[first : first + size, column : column + columns]
        column = (column + columns) % product.shape[1]
        first += size if column == 0 else 0


def weight_kernel(turned, *refs):
    partners, out = refs[:-1], refs[-1]
    rhs = jnp.concatenate([p[...] for p in partners], axis=0)
    out[...] = jnp.dot(turned[...], rhs, preferred_element_type=F32)


def final_kernel(info, *refs):
    backs, left, right = refs[:-2], refs[-2], refs[-1]
    slot, block = info[0:1, :], info[1:2, :]
    rows_dev = slot.shape[1]
    chips, part, _ = backs[0].shape
    target = (slot // part) * (chips * part) + block * part + slot % part
    values = jnp.concatenate([b[...].reshape(chips * part, -1) for b in backs], axis=0)
    hot = (iota((values.shape[0], rows_dev), 0) == target).astype(F32).astype(BF16)
    rows = lax.dot_general(
        hot, values, (((0,), (0,)), ((), ())), preferred_element_type=F32
    ).astype(BF16)
    half = left.shape[1]
    left[...] = rows[:, :half]
    right[...] = rows[:, half:]


def on_device(section_rows, lang_ids, lang_table, lang_counts, temp_num, weights):
    is_up = lax.axis_index("section") == 0
    replicas = lax.axis_size("dp")
    chips = replicas // 2
    rows_dev = lang_ids.shape[0]
    cap = 2 * rows_dev // chips
    width = section_rows.shape[2]
    own_weight = weights[0]
    ff_dev = own_weight.shape[1]

    halves = 2
    part = cap // halves
    wide = width + NOTES

    *packed, info = call(
        place_kernel,
        (
            *(sds((chips, part, wide), BF16) for _ in range(halves)),
            sds((8, rows_dev), I32),
        ),
        lang_ids.reshape(1, -1),
        lang_table.reshape(1, -1),
        lang_counts,
        section_rows[0],
        scratch=[
            pltpu.VMEM((1, rows_dev), I32),
            pltpu.VMEM((1, lang_table.shape[0]), I32),
            pltpu.VMEM(lang_counts.shape, I32),
            pltpu.VMEM((rows_dev, width), BF16),
            pltpu.SemaphoreType.DMA((4,)),
        ],
        spec=pl.BlockSpec(memory_space=pltpu.HBM),
        limit=60,
    )

    hands, received, partners = [], [], []

    def product(inputs, pieces, sizes):
        count = sum(sizes)
        hand = call(
            functools.partial(product_kernel, len(inputs), pieces),
            tuple(sds((size, ff_dev), BF16) for size in sizes),
            *inputs,
            own_weight,
            scratch=[pltpu.VMEM((count, width), BF16)],
        )
        hands.append(hand)
        received.append(across(hand))

    def back_product(g, which, shapes, *earlier):
        rows = hands[g][which].shape[0]
        partner, *outs = call(
            back_kernel,
            (sds((rows, ff_dev), BF16), *(sds(shape, F32) for shape in shapes)),
            after(received[g][which], *earlier),
            hands[g][which],
            own_weight,
        )
        partners.append(partner)
        return outs

    came, chunks = [], []
    for p in range(halves):
        packed[p] = after(packed[p], *(hands[-1] if p else ()))
        own = same_core_exchange(packed[p])
        came += [own, sibling(own)]
        cores = (1, 0) if p else (0, 1)
        chunks.append([(c, 0, r, part) for c in cores for r in range(chips)])
        rows = 2 * part * chips
        product(came[2 * p :], chunks[p], [5 * rows // 8, 3 * rows // 8] if p else [rows])
    layout = [(2 * p + which, *rest) for p in range(halves) for which, *rest in chunks[p]]
    total_rows = halves * rows
    scale, turned = call(
        functools.partial(tail_kernel, layout, [0, 1]),
        (sds((total_rows, 1), F32), sds((width, total_rows), BF16)),
        after(temp_num.reshape(1, -1), *hands[-1]),
        *came,
        scratch=[pltpu.VMEM((total_rows, width), BF16)],
    )
    def stacked(first, mine, theirs):
        return call(
            functools.partial(stack_kernel, first, len(mine)),
            sds((chips, part, width), BF16),
            scale,
            *mine,
            *theirs,
        )

    count = rows // 2
    half = (count, width // 2)
    mine, *theirs = back_product(0, 0, [(count, width), half, half], scale, *hands[1])
    stack = stacked(0, [mine], [sibling(t) for t in theirs])
    back = [same_core_exchange(stack)]
    *theirs, first = back_product(
        1, 0, [half, half, (count // 4, width)], partners[0], back[0]
    )
    theirs = [sibling(t) for t in theirs]
    (second,) = back_product(1, 1, [(3 * count // 4, width)], partners[1])
    back.append(same_core_exchange(stacked(rows + count, [first, second], theirs)))
    tile = 256
    weight_grad = pl.pallas_call(
        weight_kernel,
        out_shape=sds((width, ff_dev), F32),
        grid=(ff_dev // tile,),
        in_specs=[pl.BlockSpec((width, total_rows), lambda j: (0, 0))]
        + [pl.BlockSpec((p.shape[0], tile), lambda j: (0, j)) for p in partners],
        out_specs=pl.BlockSpec((width, tile), lambda j: (0, j)),
        compiler_params=pltpu.CompilerParams(vmem_limit_bytes=60 << 20),
        cost_estimate=pl.CostEstimate(
            flops=2 * width * total_rows * ff_dev,
            bytes_accessed=4 * width * ff_dev,
            transcendentals=0,
        ),
    )(turned, *partners)
    info = after(info, weight_grad)
    left, right = call(
        final_kernel,
        (sds((rows_dev, width // 2), BF16),) * 2,
        info,
        *back,
    )
    (right_cols,) = across([right])
    input_grad = jnp.where(is_up, left, right_cols)
    return (weight_grad[None], input_grad)


def solution(mesh):
    return jax.shard_map(
        on_device,
        mesh=mesh,
        in_specs=(
            P("section", "dp", None),
            P("dp"),
            P(),
            P("dp", None),
            P(),
            P("section", None, "dp"),
        ),
        out_specs=(P("section", None, "dp"), P("dp", "section")),
        check_vma=False,
    )
```

```python
import functools

import jax
import jax.numpy as jnp
from jax import lax
from jax.experimental import pallas as pl
from jax.experimental.pallas import tpu as pltpu
from jax.sharding import PartitionSpec as P

F32 = jnp.float32
BF16 = jnp.bfloat16
I32 = jnp.int32
NOTES = 128
VMEM = pl.BlockSpec(memory_space=pltpu.VMEM)


def sds(shape, dtype):
    return jax.ShapeDtypeStruct(shape, dtype)


def call(kernel, outs, *args, scratch=(), spec=VMEM, out_spaces=None):
    return pl.pallas_call(
        kernel,
        out_shape=outs,
        in_specs=spec if isinstance(spec, list) else [spec] * len(args),
        out_specs=(
            tuple(pl.BlockSpec(memory_space=space) for space in out_spaces)
            if out_spaces
            else jax.tree.map(lambda _: VMEM, outs)
        ),
        scratch_shapes=list(scratch),
        compiler_params=pltpu.CompilerParams(vmem_limit_bytes=12 << 20),
        cost_estimate=pl.CostEstimate(flops=1000, bytes_accessed=1000, transcendentals=0),
    )(*args)


def sibling(value):
    count = lax.axis_size("dp")
    return lax.ppermute(value, "dp", [(i, i ^ 1) for i in range(count)])


def across(values):
    return tuple(lax.ppermute(value, "section", [(0, 1), (1, 0)]) for value in values)


def same_core_exchange(value):
    count = lax.axis_size("dp")
    groups = [list(range(core, count, 2)) for core in range(2)]
    return lax.all_to_all(
        value, "dp", split_axis=0, concat_axis=0, axis_index_groups=groups, tiled=True
    )


def after(value, *others):
    return lax.optimization_barrier((value, *others))[0]


def iota(shape, dim):
    return lax.broadcasted_iota(I32, shape, dim)


def place_kernel(*refs):
    inputs, (*packed, info, weight), copies = refs[:5], refs[5:-5], refs[-5:]
    moves = [
        pltpu.make_async_copy(src, dst, copies[4].at[i])
        for i, (src, dst) in enumerate(zip(inputs, (*copies[:4], weight)))
    ]
    for move in moves:
        move.start()
    for move in moves[:4]:
        move.wait()
    ids, table, counts, rows = copies[:4]
    chips, part, _ = packed[0].shape
    width = rows.shape[1]
    chip = lax.axis_index("dp") // 2
    rows_dev = ids.shape[1]
    languages = table.shape[1]
    lang = ids[...]
    lang_hot = (iota((languages, rows_dev), 0) == lang).astype(F32)
    block = jnp.dot(table[...].astype(F32), lang_hot, preferred_element_type=F32).astype(I32)
    block_hot = iota((chips, rows_dev), 0) == block
    earlier = (iota((rows_dev, rows_dev), 0) < iota((rows_dev, rows_dev), 1)).astype(BF16)
    running = jnp.dot(
        block_hot.astype(F32).astype(BF16), earlier, preferred_element_type=F32
    )
    slot = jnp.sum(jnp.where(block_hot, running, 0.0), axis=0, keepdims=True).astype(I32)
    info[0:1, :] = slot
    info[1:2, :] = block
    info[2:, :] = jnp.zeros((info.shape[0] - 2, rows_dev), I32)
    values = counts[...].astype(F32)
    blank = jnp.zeros((1, 2 * NOTES - 2 - languages), F32)
    tail = jnp.concatenate([values[:, NOTES - 1 :], blank, jnp.zeros((1, 1), F32)], axis=1)
    head = jnp.concatenate([values[:, : NOTES - 1], jnp.zeros((1, 1), F32)], axis=1)

    def slots(target, count, first):
        hot = iota((count, rows_dev), 0) == target
        moved = jnp.dot(
            hot.astype(F32).astype(BF16), rows[...], preferred_element_type=F32
        ).astype(BF16)
        slot_lang = jnp.sum(jnp.where(hot, lang, 0), axis=1, keepdims=True).astype(F32)
        notes = jnp.where(iota((count, NOTES), 1) == NOTES - 1, slot_lang, 0.0)
        if first:
            within = iota((count, NOTES), 0) % part
            notes = notes + jnp.where(within == 0, head, 0.0) + jnp.where(within == 1, tail, 0.0)
        return moved, notes.astype(BF16)

    for p, out in enumerate(packed):
        inside = (slot // part) == p
        target = jnp.where(inside, block * part + slot % part, -1)
        moved, notes = slots(target, chips * part, p == 0)
        out[:, :, :width] = moved.reshape(chips, part, width)
        out[:, :, width:] = notes.reshape(chips, part, NOTES)
    moves[4].wait()


def load_piece(inputs, piece):
    which, first, rel, size = piece
    if rel is None:
        return inputs[which][first : first + size, :]
    return inputs[which][(lax.axis_index("dp") // 2) ^ rel]


def tail_kernel(pieces, sources, temp, *refs):
    inputs, scale_out, turned, lhs = refs[:-3], refs[-3], refs[-2], refs[-1]
    width, languages = lhs.shape[1], temp.shape[1]
    totals = [0.0, 0.0]
    for source in sources:
        for row in range(2):
            for c in range(inputs[source].shape[0]):
                totals[row] = totals[row] + inputs[source][c, row : row + 1, width:].astype(F32)
    values = temp[...].astype(F32)
    blank = jnp.zeros((1, 2 * NOTES - 2 - languages), F32)
    pads = jnp.zeros((1, 1), F32)
    numer = [
        jnp.concatenate([values[:, : NOTES - 1], pads], axis=1),
        jnp.concatenate([values[:, NOTES - 1 :], blank, pads], axis=1),
    ]
    factor = 2.0 * lax.axis_size("dp")
    lane = iota((1, NOTES), 1)
    valid = [lane < NOTES - 1, lane < languages - (NOTES - 1)]
    table = [
        jnp.where(ok, factor * n / jnp.where(ok, t, 1.0), 0.0)
        for n, t, ok in zip(numer, totals, valid)
    ]
    first = 0
    for piece in pieces:
        size = piece[3]
        values = load_piece(inputs, piece).astype(F32)
        lang = values[:, width + NOTES - 1 :].astype(I32)
        number = iota((size, NOTES), 1)
        hit = jnp.where(lang == number, table[0], 0.0) + jnp.where(
            lang - (NOTES - 1) == number, table[1], 0.0
        )
        scale = jnp.sum(hit, axis=1, keepdims=True)
        scale_out[first : first + size, :] = scale
        lhs[first : first + size, :] = (values[:, :width] * scale).astype(BF16)
        first += size
    turned[...] = lhs[...].T


def product_kernel(count, pieces, *refs):
    inputs, weight, hands, rows = refs[:count], refs[count], refs[count + 1 : -1], refs[-1]
    width = rows.shape[1]
    is_up = lax.axis_index("section") == 0
    first = 0
    for piece in pieces:
        size = piece[3]
        rows[first : first + size, :] = load_piece(inputs, piece)[:, :width]
        first += size
    tile = 512
    for j in range(0, weight.shape[1], tile):
        value = jnp.dot(rows[...], weight[:, j : j + tile], preferred_element_type=F32)
        value = jnp.where(is_up, jnp.maximum(value, 0.0), value).astype(BF16)
        first = 0
        for hand in hands:
            hand[:, j : j + tile] = value[first : first + hand.shape[0]]
            first += hand.shape[0]


def give(first, scale, total, out):
    chip = lax.axis_index("dp") // 2
    chips, part, _ = out.shape
    total = (total * scale[first : first + part * chips, :]).astype(BF16)
    for rel in range(chips):
        out[chip ^ rel] = total[rel * part : (rel + 1) * part]


def stack_kernel(first, scale, mine, left, right, out):
    theirs = jnp.concatenate([left[...], right[...]], axis=1)
    give(first, scale, mine[...] + theirs.astype(F32), out)


def mask_and_leave(recv, hand, value, partner, done):
    is_up = lax.axis_index("section") == 0
    masked = is_up & (hand[...] <= 0)
    value[...] = jnp.where(masked, jnp.zeros_like(recv), recv[...])
    leave = pltpu.make_async_copy(value, partner, done)
    leave.start()
    return leave


def product_of(value, weight):
    return lax.dot_general(value, weight, (((1,), (1,)), ((), ())), preferred_element_type=F32)


def spread(product, theirs_first, mine, left, right):
    count, columns = left.shape
    theirs = 0 if theirs_first else mine.shape[0]
    left[...] = product[theirs : theirs + count, :columns].astype(BF16)
    right[...] = product[theirs : theirs + count, columns:].astype(BF16)
    own = count if theirs_first else 0
    mine[...] = product[own : own + mine.shape[0]]


def back_kernel(recv, hand, weight, partner, mine, left, right, value, done):
    leave = mask_and_leave(recv, hand, value, partner, done)
    spread(product_of(value[...], weight[...]), False, mine, left, right)
    leave.wait()


def fetch_kernel(recv, hand, weight, partner, mine, left, right, value, done, kept, came):
    tile = weight.shape[1] // 4
    cuts = [slice(i * tile, (i + 1) * tile) for i in range(4)]
    moves = [
        pltpu.make_async_copy(weight.at[:, cut], kept.at[:, cut], came.at[i])
        for i, cut in enumerate(cuts)
    ]
    for move in moves:
        move.start()
    leave = mask_and_leave(recv, hand, value, partner, done)
    product = 0.0
    for move, cut in zip(moves, cuts):
        move.wait()
        product = product + product_of(value[:, cut], kept[:, cut])
    spread(product, True, mine, left, right)
    leave.wait()


def keep_kernel(weight, token, kept, done):
    move = pltpu.make_async_copy(weight, kept, done)
    move.start()
    move.wait()


def last_kernel(first, recv, hand, weight, scale, mine, left, right, partner, out, value, done):
    leave = mask_and_leave(recv, hand, value, partner, done)
    product = product_of(value[...], weight[...])
    theirs = jnp.concatenate([left[...], right[...]], axis=1)
    total = jnp.concatenate([mine[...], product], axis=0) + theirs.astype(F32)
    give(first, scale, total, out)
    leave.wait()


def weight_kernel(turned, *refs):
    partners, out = refs[:-1], refs[-1]
    rhs = jnp.concatenate([p[...] for p in partners], axis=0)
    out[...] = jnp.dot(turned[...], rhs, preferred_element_type=F32)


def unpack(half, info, back):
    slot, block = info[0:1, :], info[1:2, :]
    chips, part, width = back.shape
    target = jnp.where(slot // part == half, block * part + slot % part, -1)
    hot = (iota((chips * part, target.shape[1]), 0) == target).astype(F32).astype(BF16)
    return lax.dot_general(
        hot,
        back[...].reshape(chips * part, width),
        (((0,), (0,)), ((), ())),
        preferred_element_type=F32,
    )


def unpack_kernel(info, back, out):
    out[...] = unpack(0, info, back).astype(BF16)


def final_kernel(info, back, early, left, right):
    rows = (unpack(1, info, back) + early[...].astype(F32)).astype(BF16)
    half = left.shape[1]
    left[...] = rows[:, :half]
    right[...] = rows[:, half:]


def on_device(section_rows, lang_ids, lang_table, lang_counts, temp_num, weights):
    is_up = lax.axis_index("section") == 0
    replicas = lax.axis_size("dp")
    chips = replicas // 2
    rows_dev = lang_ids.shape[0]
    cap = 2 * rows_dev // chips
    width = section_rows.shape[2]
    own_weight = weights[0]
    ff_dev = own_weight.shape[1]

    halves = 2
    part = cap // halves
    wide = width + NOTES

    *packed, info, fast_weight = call(
        place_kernel,
        (
            *(sds((chips, part, wide), BF16) for _ in range(halves)),
            sds((8, rows_dev), I32),
            pltpu.VMEM(own_weight.shape, BF16),
        ),
        *(
            pltpu.with_memory_space_constraint(value, pltpu.HBM)
            for value in (
                lang_ids.reshape(1, -1),
                lang_table.reshape(1, -1),
                lang_counts,
                section_rows[0],
                own_weight,
            )
        ),
        scratch=[
            pltpu.VMEM((1, rows_dev), I32),
            pltpu.VMEM((1, lang_table.shape[0]), I32),
            pltpu.VMEM(lang_counts.shape, I32),
            pltpu.VMEM((rows_dev, width), BF16),
            pltpu.SemaphoreType.DMA((5,)),
        ],
        spec=pl.BlockSpec(memory_space=pltpu.HBM),
    )

    hands, received, partners = [], [], []

    def product(inputs, pieces, sizes):
        count = sum(sizes)
        hand = call(
            functools.partial(product_kernel, len(inputs), pieces),
            tuple(sds((size, ff_dev), BF16) for size in sizes),
            *inputs,
            fast_weight,
            scratch=[pltpu.VMEM((count, width), BF16)],
        )
        hands.append(hand)
        received.append(across(hand))

    came, chunks = [], []
    for p in range(halves):
        packed[p] = after(packed[p], *(hands[-1] if p else ()))
        own = same_core_exchange(packed[p])
        came += [own, sibling(own)]
        cores = (1, 0) if p else (0, 1)
        chunks.append([(c, 0, r, part) for c in cores for r in range(chips)])
        rows = 2 * part * chips
        product(came[2 * p :], chunks[p], [5 * rows // 8, 3 * rows // 8] if p else [rows])
    layout = [(2 * p + which, *rest) for p in range(halves) for which, *rest in chunks[p]]
    total_rows = halves * rows
    scale, turned = call(
        functools.partial(tail_kernel, layout, [0, 1]),
        (sds((total_rows, 1), F32), sds((width, total_rows), BF16)),
        after(temp_num.reshape(1, -1), *hands[-1]),
        *came,
        scratch=[pltpu.VMEM((total_rows, width), BF16)],
    )
    count = rows // 2
    half = sds((count, width // 2), BF16)
    late_rows = [hand.shape[0] for hand in hands[1]]

    def room(size):
        return [pltpu.VMEM((size, ff_dev), BF16), pltpu.SemaphoreType.DMA]

    def backed(kernel, size, outs, args, scratch=(), specs=VMEM):
        partner, *rest = call(
            kernel,
            (pltpu.HBM((size, ff_dev), BF16), *outs),
            *args,
            scratch=[*room(size), *scratch],
            out_spaces=(pltpu.HBM, *(pltpu.VMEM for _ in outs)),
            spec=specs,
        )
        partners.append(partner)
        return rest

    mine, left, right = backed(
        back_kernel,
        rows,
        [sds((count, width), F32), half, half],
        [after(received[0][0], scale, *hands[1]), hands[0][0], fast_weight],
    )
    stack = call(
        functools.partial(stack_kernel, 0),
        sds((chips, part, width), BF16),
        scale,
        mine,
        sibling(left),
        sibling(right),
    )
    early = call(
        unpack_kernel,
        sds((rows_dev, width), BF16),
        info,
        same_core_exchange(stack),
    )
    far_weight = pltpu.with_memory_space_constraint(own_weight, pltpu.HBM)
    in_hbm = pl.BlockSpec(memory_space=pltpu.HBM)
    mine, left, right = backed(
        fetch_kernel,
        late_rows[0],
        [sds((late_rows[0] - count, width), F32), half, half],
        [after(received[1][0], partners[0], stack), hands[1][0], far_weight],
        scratch=[pltpu.VMEM(own_weight.shape, BF16), pltpu.SemaphoreType.DMA((4,))],
        specs=[VMEM, VMEM, in_hbm],
    )
    (kept,) = call(
        keep_kernel,
        (pltpu.VMEM(own_weight.shape, BF16),),
        far_weight,
        after(info, early, mine),
        scratch=[pltpu.SemaphoreType.DMA],
        spec=[in_hbm, VMEM],
    )
    (stack,) = backed(
        functools.partial(last_kernel, rows + count),
        late_rows[1],
        [sds((chips, part, width), BF16)],
        [
            after(received[1][1], partners[1], kept),
            hands[1][1],
            kept,
            scale,
            mine,
            sibling(left),
            sibling(right),
        ],
    )
    late = same_core_exchange(stack)
    tile = 256
    weight_grad = pl.pallas_call(
        weight_kernel,
        out_shape=sds((width, ff_dev), F32),
        grid=(ff_dev // tile,),
        in_specs=[pl.BlockSpec((width, total_rows), lambda j: (0, 0))]
        + [pl.BlockSpec((p.shape[0], tile), lambda j: (0, j)) for p in partners],
        out_specs=pl.BlockSpec((width, tile), lambda j: (0, j)),
        compiler_params=pltpu.CompilerParams(vmem_limit_bytes=60 << 20),
        cost_estimate=pl.CostEstimate(
            flops=2 * width * total_rows * ff_dev,
            bytes_accessed=4 * width * ff_dev,
            transcendentals=0,
        ),
    )(turned, *partners)
    info = after(info, weight_grad)
    left, right = call(
        final_kernel,
        (sds((rows_dev, width // 2), BF16),) * 2,
        info,
        late,
        early,
    )
    (right_cols,) = across([right])
    input_grad = jnp.where(is_up, left, right_cols)
    return (weight_grad[None], input_grad)


def solution(mesh):
    return jax.shard_map(
        on_device,
        mesh=mesh,
        in_specs=(
            P("section", "dp", None),
            P("dp"),
            P(),
            P("dp", None),
            P(),
            P("section", None, "dp"),
        ),
        out_specs=(P("section", None, "dp"), P("dp", "section")),
        check_vma=False,
    )
```

```python
import functools

import jax
import jax.numpy as jnp
from jax import lax
from jax.experimental import pallas as pl
from jax.experimental.pallas import tpu as pltpu
from jax.sharding import PartitionSpec as P

F32 = jnp.float32
BF16 = jnp.bfloat16
I32 = jnp.int32
NOTES = 128
VMEM = pl.BlockSpec(memory_space=pltpu.VMEM)


def sds(shape, dtype):
    return jax.ShapeDtypeStruct(shape, dtype)


def call(kernel, outs, *args, scratch=(), spec=VMEM, out_spaces=None, aliases=None):
    return pl.pallas_call(
        kernel,
        out_shape=outs,
        in_specs=spec if isinstance(spec, list) else [spec] * len(args),
        out_specs=(
            tuple(pl.BlockSpec(memory_space=space) for space in out_spaces)
            if out_spaces
            else jax.tree.map(lambda _: VMEM, outs)
        ),
        scratch_shapes=list(scratch),
        input_output_aliases=aliases or {},
        compiler_params=pltpu.CompilerParams(vmem_limit_bytes=12 << 20),
        cost_estimate=pl.CostEstimate(flops=1000, bytes_accessed=1000, transcendentals=0),
    )(*args)


def sibling(value):
    count = lax.axis_size("dp")
    return lax.ppermute(value, "dp", [(i, i ^ 1) for i in range(count)])


def across(values):
    return tuple(lax.ppermute(value, "section", [(0, 1), (1, 0)]) for value in values)


def same_core_exchange(value):
    count = lax.axis_size("dp")
    groups = [list(range(core, count, 2)) for core in range(2)]
    return lax.all_to_all(
        value, "dp", split_axis=0, concat_axis=0, axis_index_groups=groups, tiled=True
    )


def after(value, *others):
    return lax.optimization_barrier((value, *others))[0]


def iota(shape, dim):
    return lax.broadcasted_iota(I32, shape, dim)


def place_kernel(*refs):
    inputs, (*packed, info, weight), copies = refs[:5], refs[5:-5], refs[-5:]
    moves = [
        pltpu.make_async_copy(src, dst, copies[4].at[i])
        for i, (src, dst) in enumerate(zip(inputs, (*copies[:4], weight)))
    ]
    for move in moves:
        move.start()
    for move in moves[:4]:
        move.wait()
    ids, table, counts, rows = copies[:4]
    chips, part, _ = packed[0].shape
    width = rows.shape[1]
    chip = lax.axis_index("dp") // 2
    rows_dev = ids.shape[1]
    languages = table.shape[1]
    lang = ids[...]
    lang_hot = (iota((languages, rows_dev), 0) == lang).astype(F32)
    block = jnp.dot(table[...].astype(F32), lang_hot, preferred_element_type=F32).astype(I32)
    block_hot = iota((chips, rows_dev), 0) == block
    earlier = (iota((rows_dev, rows_dev), 0) < iota((rows_dev, rows_dev), 1)).astype(BF16)
    running = jnp.dot(
        block_hot.astype(F32).astype(BF16), earlier, preferred_element_type=F32
    )
    slot = jnp.sum(jnp.where(block_hot, running, 0.0), axis=0, keepdims=True).astype(I32)
    info[0:1, :] = slot
    info[1:2, :] = block
    info[2:, :] = jnp.zeros((info.shape[0] - 2, rows_dev), I32)
    values = counts[...].astype(F32)
    blank = jnp.zeros((1, 2 * NOTES - 2 - languages), F32)
    tail = jnp.concatenate([values[:, NOTES - 1 :], blank, jnp.zeros((1, 1), F32)], axis=1)
    head = jnp.concatenate([values[:, : NOTES - 1], jnp.zeros((1, 1), F32)], axis=1)

    def slots(target, count, first):
        hot = iota((count, rows_dev), 0) == target
        moved = jnp.dot(
            hot.astype(F32).astype(BF16), rows[...], preferred_element_type=F32
        ).astype(BF16)
        slot_lang = jnp.sum(jnp.where(hot, lang, 0), axis=1, keepdims=True).astype(F32)
        notes = jnp.where(iota((count, NOTES), 1) == NOTES - 1, slot_lang, 0.0)
        if first:
            within = iota((count, NOTES), 0) % part
            notes = notes + jnp.where(within == 0, head, 0.0) + jnp.where(within == 1, tail, 0.0)
        return moved, notes.astype(BF16)

    for p, out in enumerate(packed):
        inside = (slot // part) == p
        target = jnp.where(inside, block * part + slot % part, -1)
        moved, notes = slots(target, chips * part, p == 0)
        out[:, :, :width] = moved.reshape(chips, part, width)
        out[:, :, width:] = notes.reshape(chips, part, NOTES)
    moves[4].wait()


def load_piece(inputs, piece):
    which, first, rel, size = piece
    if rel is None:
        return inputs[which][first : first + size, :]
    return inputs[which][(lax.axis_index("dp") // 2) ^ rel]


def tail_kernel(pieces, sources, temp, *refs):
    inputs, scale_out, turned, lhs = refs[:-3], refs[-3], refs[-2], refs[-1]
    width, languages = lhs.shape[1], temp.shape[1]
    totals = [0.0, 0.0]
    for source in sources:
        for row in range(2):
            for c in range(inputs[source].shape[0]):
                totals[row] = totals[row] + inputs[source][c, row : row + 1, width:].astype(F32)
    values = temp[...].astype(F32)
    blank = jnp.zeros((1, 2 * NOTES - 2 - languages), F32)
    pads = jnp.zeros((1, 1), F32)
    numer = [
        jnp.concatenate([values[:, : NOTES - 1], pads], axis=1),
        jnp.concatenate([values[:, NOTES - 1 :], blank, pads], axis=1),
    ]
    factor = 2.0 * lax.axis_size("dp")
    lane = iota((1, NOTES), 1)
    valid = [lane < NOTES - 1, lane < languages - (NOTES - 1)]
    table = [
        jnp.where(ok, factor * n / jnp.where(ok, t, 1.0), 0.0)
        for n, t, ok in zip(numer, totals, valid)
    ]
    first = 0
    for piece in pieces:
        size = piece[3]
        values = load_piece(inputs, piece).astype(F32)
        lang = values[:, width + NOTES - 1 :].astype(I32)
        number = iota((size, NOTES), 1)
        hit = jnp.where(lang == number, table[0], 0.0) + jnp.where(
            lang - (NOTES - 1) == number, table[1], 0.0
        )
        scale = jnp.sum(hit, axis=1, keepdims=True)
        scale_out[first : first + size, :] = scale
        lhs[first : first + size, :] = (values[:, :width] * scale).astype(BF16)
        first += size
    turned[...] = lhs[...].T


def product_kernel(count, pieces, at, *refs):
    inputs, weight = refs[:count], refs[count]
    hands, rows = refs[count + 1 : -1], refs[-1]
    if at:
        hands = hands[1:]
    width = rows.shape[1]
    is_up = lax.axis_index("section") == 0
    first = 0
    for piece in pieces:
        size = piece[3]
        rows[first : first + size, :] = load_piece(inputs, piece)[:, :width]
        first += size
    tile = 512
    for j in range(0, weight.shape[1], tile):
        value = jnp.dot(rows[...], weight[:, j : j + tile], preferred_element_type=F32)
        value = jnp.where(is_up, jnp.maximum(value, 0.0), value).astype(BF16)
        first = 0
        for hand in hands:
            size = min(hand.shape[0], value.shape[0])
            hand[at : at + size, j : j + tile] = value[first : first + size]
            first += size


def give(first, scale, total, *outs):
    chip = lax.axis_index("dp") // 2
    chips, part, columns = outs[0].shape
    total = (total * scale[first : first + part * chips, :]).astype(BF16)
    for i, out in enumerate(outs):
        for rel in range(chips):
            out[chip ^ rel] = total[
                rel * part : (rel + 1) * part, i * columns : (i + 1) * columns
            ]


def stack_kernel(first, scale, mine, left, right, out):
    theirs = jnp.concatenate([left[...], right[...]], axis=1)
    give(first, scale, mine[...] + theirs.astype(F32), out)


def mask_and_leave(recv, hand, value, partner, done):
    is_up = lax.axis_index("section") == 0
    masked = is_up & (hand[...] <= 0)
    value[...] = jnp.where(masked, jnp.zeros_like(recv), recv[...])
    leave = pltpu.make_async_copy(value, partner, done)
    leave.start()
    return leave


def product_of(value, weight):
    return lax.dot_general(value, weight, (((1,), (1,)), ((), ())), preferred_element_type=F32)


def spread(product, theirs_first, mine, left, right):
    count, columns = left.shape
    theirs = 0 if theirs_first else mine.shape[0]
    left[...] = product[theirs : theirs + count, :columns].astype(BF16)
    right[...] = product[theirs : theirs + count, columns:].astype(BF16)
    own = count if theirs_first else 0
    mine[...] = product[own : own + mine.shape[0]]


def back_kernel(recv, hand, weight, partner, mine, left, right, value, done):
    leave = mask_and_leave(recv, hand, value, partner, done)
    spread(product_of(value[...], weight[...]), False, mine, left, right)
    leave.wait()


def fetch_kernel(recv, hand, weight, partner, mine, left, right, value, done, kept, came):
    tile = weight.shape[1] // 4
    cuts = [slice(i * tile, (i + 1) * tile) for i in range(4)]
    moves = [
        pltpu.make_async_copy(weight.at[:, cut], kept.at[:, cut], came.at[i])
        for i, cut in enumerate(cuts)
    ]
    for move in moves:
        move.start()
    leave = mask_and_leave(recv, hand, value, partner, done)
    product = 0.0
    for move, cut in zip(moves, cuts):
        move.wait()
        product = product + product_of(value[:, cut], kept[:, cut])
    spread(product, True, mine, left, right)
    leave.wait()


def keep_kernel(weight, token, kept, done):
    move = pltpu.make_async_copy(weight, kept, done)
    move.start()
    move.wait()


def last_kernel(first, recv, hand, weight, scale, mine, left, right, partner, *rest):
    outs, value, done = rest[:-2], rest[-2], rest[-1]
    leave = mask_and_leave(recv, hand, value, partner, done)
    product = product_of(value[...], weight[...])
    theirs = jnp.concatenate([left[...], right[...]], axis=1)
    total = jnp.concatenate([mine[...], product], axis=0) + theirs.astype(F32)
    give(first, scale, total, *outs)
    leave.wait()


def weight_kernel(count, turned, *refs):
    partners, out = refs[:count], refs[-1]
    rhs = jnp.concatenate([p[...] for p in partners], axis=0)
    out[...] = jnp.dot(turned[...], rhs, preferred_element_type=F32)


def unpack(half, info, back):
    slot, block = info[0:1, :], info[1:2, :]
    chips, part, width = back.shape
    target = jnp.where(slot // part == half, block * part + slot % part, -1)
    hot = (iota((chips * part, target.shape[1]), 0) == target).astype(F32).astype(BF16)
    return lax.dot_general(
        hot,
        back[...].reshape(chips * part, width),
        (((0,), (0,)), ((), ())),
        preferred_element_type=F32,
    )


def unpack_kernel(info, back, left, right):
    rows = unpack(0, info, back).astype(BF16)
    half = left.shape[1]
    left[...] = rows[:, :half]
    right[...] = rows[:, half:]


def choose_kernel(left, right, out):
    is_up = lax.axis_index("section") == 0
    out[...] = jnp.where(is_up, left[...], right[...])


def final_kernel(info, back, left, right, out):
    is_up = lax.axis_index("section") == 0
    early = jnp.where(is_up, left[...], right[...]).astype(F32)
    out[...] = (unpack(1, info, back) + early).astype(BF16)


def on_device(section_rows, lang_ids, lang_table, lang_counts, temp_num, weights):
    is_up = lax.axis_index("section") == 0
    replicas = lax.axis_size("dp")
    chips = replicas // 2
    rows_dev = lang_ids.shape[0]
    cap = 2 * rows_dev // chips
    width = section_rows.shape[2]
    own_weight = weights[0]
    ff_dev = own_weight.shape[1]

    halves = 2
    part = cap // halves
    wide = width + NOTES

    *packed, info, fast_weight = call(
        place_kernel,
        (
            *(sds((chips, part, wide), BF16) for _ in range(halves)),
            sds((8, rows_dev), I32),
            pltpu.VMEM(own_weight.shape, BF16),
        ),
        *(
            pltpu.with_memory_space_constraint(value, pltpu.HBM)
            for value in (
                lang_ids.reshape(1, -1),
                lang_table.reshape(1, -1),
                lang_counts,
                section_rows[0],
                own_weight,
            )
        ),
        scratch=[
            pltpu.VMEM((1, rows_dev), I32),
            pltpu.VMEM((1, lang_table.shape[0]), I32),
            pltpu.VMEM(lang_counts.shape, I32),
            pltpu.VMEM((rows_dev, width), BF16),
            pltpu.SemaphoreType.DMA((5,)),
        ],
        spec=pl.BlockSpec(memory_space=pltpu.HBM),
    )

    hands, received, partners = [], [], []

    def product(inputs, pieces, sizes, at=0, sofar=()):
        return call(
            functools.partial(product_kernel, len(inputs), pieces, at),
            tuple(sds((size, ff_dev), BF16) for size in sizes),
            *inputs,
            fast_weight,
            *sofar,
            scratch=[pltpu.VMEM((sum(piece[3] for piece in pieces), width), BF16)],
            aliases={len(inputs) + 1: 0} if sofar else {},
        )

    came, chunks = [], []
    for p in range(halves):
        packed[p] = after(packed[p], *(hands[-1] if p else ()))
        own = same_core_exchange(packed[p])
        came += [own, sibling(own)]
        cores = (1, 0) if p else (0, 1)
        chunks.append([(c, 0, r, part) for c in cores for r in range(chips)])
        rows = 2 * part * chips
        if p:
            hand = product(came[2:], chunks[p], [5 * rows // 8, 3 * rows // 8])
        else:
            mine = product(came[:1], chunks[p][:chips], [rows])
            theirs = [(0, *rest) for _, *rest in chunks[p][chips:]]
            hand = product(came[1:], theirs, [rows], rows // 2, mine)
        hands.append(hand)
        received.append(across(hand))
    layout = [(2 * p + which, *rest) for p in range(halves) for which, *rest in chunks[p]]
    total_rows = halves * rows
    scale, turned = call(
        functools.partial(tail_kernel, layout, [0, 1]),
        (sds((total_rows, 1), F32), sds((width, total_rows), BF16)),
        after(temp_num.reshape(1, -1), *hands[-1]),
        *came,
        scratch=[pltpu.VMEM((total_rows, width), BF16)],
    )
    count = rows // 2
    half = sds((count, width // 2), BF16)
    late_rows = [hand.shape[0] for hand in hands[1]]

    def room(size):
        return [pltpu.VMEM((size, ff_dev), BF16), pltpu.SemaphoreType.DMA]

    def backed(kernel, size, outs, args, scratch=(), specs=VMEM):
        partner, *rest = call(
            kernel,
            (pltpu.HBM((size, ff_dev), BF16), *outs),
            *args,
            scratch=[*room(size), *scratch],
            out_spaces=(pltpu.HBM, *(pltpu.VMEM for _ in outs)),
            spec=specs,
        )
        partners.append(partner)
        return rest

    mine, left, right = backed(
        back_kernel,
        rows,
        [sds((count, width), F32), half, half],
        [after(received[0][0], scale, *hands[1]), hands[0][0], fast_weight],
    )
    stack = call(
        functools.partial(stack_kernel, 0),
        sds((chips, part, width), BF16),
        scale,
        mine,
        sibling(left),
        sibling(right),
    )
    early_left, early_right = call(
        unpack_kernel,
        (sds((rows_dev, width // 2), BF16),) * 2,
        info,
        same_core_exchange(stack),
    )
    far_weight = pltpu.with_memory_space_constraint(own_weight, pltpu.HBM)
    in_hbm = pl.BlockSpec(memory_space=pltpu.HBM)
    mine, left, right = backed(
        fetch_kernel,
        late_rows[0],
        [sds((late_rows[0] - count, width), F32), half, half],
        [after(received[1][0], partners[0], stack), hands[1][0], far_weight],
        scratch=[pltpu.VMEM(own_weight.shape, BF16), pltpu.SemaphoreType.DMA((4,))],
        specs=[VMEM, VMEM, in_hbm],
    )
    (kept,) = call(
        keep_kernel,
        (pltpu.VMEM(own_weight.shape, BF16),),
        far_weight,
        after(info, early_left, mine),
        scratch=[pltpu.SemaphoreType.DMA],
        spec=[in_hbm, VMEM],
    )
    late_left, late_right = backed(
        functools.partial(last_kernel, rows + count),
        late_rows[1],
        [sds((chips, part, width // 2), BF16)] * 2,
        [
            after(received[1][1], partners[1], kept),
            hands[1][1],
            kept,
            scale,
            mine,
            sibling(left),
            sibling(right),
        ],
    )
    (late_recv,) = across([late_right])
    tile = 256
    first_tiles = ff_dev // tile // 4

    def weight_part(start, steps, sofar=()):
        return pl.pallas_call(
            functools.partial(weight_kernel, len(partners)),
            out_shape=sds((width, ff_dev), F32),
            grid=(steps,),
            in_specs=[pl.BlockSpec((width, total_rows), lambda j: (0, 0))]
            + [pl.BlockSpec((p.shape[0], tile), lambda j: (0, start + j)) for p in partners]
            + [pl.BlockSpec(memory_space=pl.ANY) for _ in sofar],
            out_specs=pl.BlockSpec((width, tile), lambda j: (0, start + j)),
            input_output_aliases={1 + len(partners): 0} if sofar else {},
            compiler_params=pltpu.CompilerParams(vmem_limit_bytes=60 << 20),
            cost_estimate=pl.CostEstimate(
                flops=1000, bytes_accessed=1000, transcendentals=0
            ),
        )(turned, *partners, *sofar)

    weight_grad = weight_part(0, first_tiles)
    late_recv = after(late_recv, weight_grad)
    late = call(choose_kernel, sds((chips, part, width // 2), BF16), late_left, late_recv)
    late = same_core_exchange(late)
    (early_recv,) = across([after(early_right, late_recv)])
    weight_grad = weight_part(first_tiles, ff_dev // tile - first_tiles, [weight_grad])
    info = after(info, weight_grad)
    input_grad = pl.pallas_call(
        final_kernel,
        out_shape=sds((rows_dev, width // 2), BF16),
        compiler_params=pltpu.CompilerParams(vmem_limit_bytes=12 << 20),
        cost_estimate=pl.CostEstimate(flops=1000, bytes_accessed=1000, transcendentals=0),
    )(info, late, early_left, early_recv)
    return (weight_grad[None], input_grad)


def solution(mesh):
    return jax.shard_map(
        on_device,
        mesh=mesh,
        in_specs=(
            P("section", "dp", None),
            P("dp"),
            P(),
            P("dp", None),
            P(),
            P("section", None, "dp"),
        ),
        out_specs=(P("section", None, "dp"), P("dp", "section")),
        check_vma=False,
    )
```

```python
import functools

import jax
import jax.numpy as jnp
from jax import lax
from jax.experimental import pallas as pl
from jax.experimental.pallas import tpu as pltpu
from jax.sharding import PartitionSpec as P

F32 = jnp.float32
BF16 = jnp.bfloat16
I32 = jnp.int32
NOTES = 128
VMEM = pl.BlockSpec(memory_space=pltpu.VMEM)


def sds(shape, dtype):
    return jax.ShapeDtypeStruct(shape, dtype)


def call(kernel, outs, *args, scratch=(), spec=VMEM, out_spaces=None, aliases=None):
    return pl.pallas_call(
        kernel,
        out_shape=outs,
        in_specs=spec if isinstance(spec, list) else [spec] * len(args),
        out_specs=(
            tuple(pl.BlockSpec(memory_space=space) for space in out_spaces)
            if out_spaces
            else jax.tree.map(lambda _: VMEM, outs)
        ),
        scratch_shapes=list(scratch),
        input_output_aliases=aliases or {},
        compiler_params=pltpu.CompilerParams(vmem_limit_bytes=12 << 20),
        cost_estimate=pl.CostEstimate(flops=1000, bytes_accessed=1000, transcendentals=0),
    )(*args)


def sibling(value):
    count = lax.axis_size("dp")
    return lax.ppermute(value, "dp", [(i, i ^ 1) for i in range(count)])


def across(values):
    return tuple(lax.ppermute(value, "section", [(0, 1), (1, 0)]) for value in values)


def same_core_exchange(value):
    count = lax.axis_size("dp")
    groups = [list(range(core, count, 2)) for core in range(2)]
    return lax.all_to_all(
        value, "dp", split_axis=0, concat_axis=0, axis_index_groups=groups, tiled=True
    )


def after(value, *others):
    return lax.optimization_barrier((value, *others))[0]


def iota(shape, dim):
    return lax.broadcasted_iota(I32, shape, dim)


def place_kernel(*refs):
    inputs, (*packed, info, weight), copies = refs[:5], refs[5:-5], refs[-5:]
    moves = [
        pltpu.make_async_copy(src, dst, copies[4].at[i])
        for i, (src, dst) in enumerate(zip(inputs, (*copies[:4], weight)))
    ]
    for move in moves:
        move.start()
    for move in moves[:3]:
        move.wait()
    ids, table, counts, rows = copies[:4]
    chips, part, _ = packed[0].shape
    width = rows.shape[1]
    chip = lax.axis_index("dp") // 2
    rows_dev = ids.shape[1]
    languages = table.shape[1]
    lang = ids[...]
    lang_hot = (iota((languages, rows_dev), 0) == lang).astype(F32)
    block = jnp.dot(table[...].astype(F32), lang_hot, preferred_element_type=F32).astype(I32)
    block_hot = iota((chips, rows_dev), 0) == block
    earlier = (iota((rows_dev, rows_dev), 0) < iota((rows_dev, rows_dev), 1)).astype(BF16)
    running = jnp.dot(
        block_hot.astype(F32).astype(BF16), earlier, preferred_element_type=F32
    )
    slot = jnp.sum(jnp.where(block_hot, running, 0.0), axis=0, keepdims=True).astype(I32)
    info[0:1, :] = slot
    info[1:2, :] = block
    info[2:, :] = jnp.zeros((info.shape[0] - 2, rows_dev), I32)
    values = counts[...].astype(F32)
    blank = jnp.zeros((1, 2 * NOTES - 2 - languages), F32)
    tail = jnp.concatenate([values[:, NOTES - 1 :], blank, jnp.zeros((1, 1), F32)], axis=1)
    head = jnp.concatenate([values[:, : NOTES - 1], jnp.zeros((1, 1), F32)], axis=1)

    def slots(target, count, first):
        hot = iota((count, rows_dev), 0) == target
        moved = jnp.dot(
            hot.astype(F32).astype(BF16), rows[...], preferred_element_type=F32
        ).astype(BF16)
        slot_lang = jnp.sum(jnp.where(hot, lang, 0), axis=1, keepdims=True).astype(F32)
        notes = jnp.where(iota((count, NOTES), 1) == NOTES - 1, slot_lang, 0.0)
        if first:
            within = iota((count, NOTES), 0) % part
            notes = notes + jnp.where(within == 0, head, 0.0) + jnp.where(within == 1, tail, 0.0)
        return moved, notes.astype(BF16)

    moves[3].wait()
    for p, out in enumerate(packed):
        inside = (slot // part) == p
        target = jnp.where(inside, block * part + slot % part, -1)
        moved, notes = slots(target, chips * part, p == 0)
        out[:, :, :width] = moved.reshape(chips, part, width)
        out[:, :, width:] = notes.reshape(chips, part, NOTES)
    moves[4].wait()


def load_piece(inputs, piece):
    which, first, rel, size = piece
    if rel is None:
        return inputs[which][first : first + size, :]
    return inputs[which][(lax.axis_index("dp") // 2) ^ rel]


def tail_kernel(pieces, sources, temp, *refs):
    inputs, scale_out, turned, lhs = refs[:-3], refs[-3], refs[-2], refs[-1]
    width, languages = lhs.shape[1], temp.shape[1]
    totals = [0.0, 0.0]
    for source in sources:
        for row in range(2):
            for c in range(inputs[source].shape[0]):
                totals[row] = totals[row] + inputs[source][c, row : row + 1, width:].astype(F32)
    values = temp[...].astype(F32)
    blank = jnp.zeros((1, 2 * NOTES - 2 - languages), F32)
    pads = jnp.zeros((1, 1), F32)
    numer = [
        jnp.concatenate([values[:, : NOTES - 1], pads], axis=1),
        jnp.concatenate([values[:, NOTES - 1 :], blank, pads], axis=1),
    ]
    factor = 2.0 * lax.axis_size("dp")
    lane = iota((1, NOTES), 1)
    valid = [lane < NOTES - 1, lane < languages - (NOTES - 1)]
    table = [
        jnp.where(ok, factor * n / jnp.where(ok, t, 1.0), 0.0)
        for n, t, ok in zip(numer, totals, valid)
    ]
    first = 0
    for piece in pieces:
        size = piece[3]
        values = load_piece(inputs, piece).astype(F32)
        lang = values[:, width + NOTES - 1 :].astype(I32)
        number = iota((size, NOTES), 1)
        hit = jnp.where(lang == number, table[0], 0.0) + jnp.where(
            lang - (NOTES - 1) == number, table[1], 0.0
        )
        scale = jnp.sum(hit, axis=1, keepdims=True)
        scale_out[first : first + size, :] = scale
        lhs[first : first + size, :] = (values[:, :width] * scale).astype(BF16)
        first += size
    turned[...] = lhs[...].T


def product_kernel(count, pieces, at, *refs):
    inputs, weight = refs[:count], refs[count]
    hands, rows = refs[count + 1 : -1], refs[-1]
    if at:
        hands = hands[1:]
    width = rows.shape[1]
    is_up = lax.axis_index("section") == 0
    first = 0
    for piece in pieces:
        size = piece[3]
        rows[first : first + size, :] = load_piece(inputs, piece)[:, :width]
        first += size
    tile = 512
    for j in range(0, weight.shape[1], tile):
        value = jnp.dot(rows[...], weight[:, j : j + tile], preferred_element_type=F32)
        value = jnp.where(is_up, jnp.maximum(value, 0.0), value).astype(BF16)
        first = 0
        for hand in hands:
            size = min(hand.shape[0], value.shape[0])
            hand[at : at + size, j : j + tile] = value[first : first + size]
            first += size


def give(first, scale, total, *outs):
    chip = lax.axis_index("dp") // 2
    chips, part, columns = outs[0].shape
    total = (total * scale[first : first + part * chips, :]).astype(BF16)
    for i, out in enumerate(outs):
        for rel in range(chips):
            out[chip ^ rel] = total[
                rel * part : (rel + 1) * part, i * columns : (i + 1) * columns
            ]


def stack_kernel(first, scale, mine, left, right, out):
    theirs = jnp.concatenate([left[...], right[...]], axis=1)
    give(first, scale, mine[...] + theirs.astype(F32), out)


def mask_and_leave(recv, hand, value, partner, done):
    is_up = lax.axis_index("section") == 0
    masked = is_up & (hand[...] <= 0)
    value[...] = jnp.where(masked, jnp.zeros_like(recv), recv[...])
    leave = pltpu.make_async_copy(value, partner, done)
    leave.start()
    return leave


def product_of(value, weight):
    return lax.dot_general(value, weight, (((1,), (1,)), ((), ())), preferred_element_type=F32)


def spread(product, theirs_first, mine, left, right):
    count, columns = left.shape
    theirs = 0 if theirs_first else mine.shape[0]
    left[...] = product[theirs : theirs + count, :columns].astype(BF16)
    right[...] = product[theirs : theirs + count, columns:].astype(BF16)
    own = count if theirs_first else 0
    mine[...] = product[own : own + mine.shape[0]]


def back_kernel(recv, hand, weight, partner, mine, left, right, value, done):
    leave = mask_and_leave(recv, hand, value, partner, done)
    spread(product_of(value[...], weight[...]), False, mine, left, right)
    leave.wait()


def fetch_kernel(recv, hand, weight, partner, mine, left, right, value, done, kept, came):
    tile = weight.shape[1] // 4
    cuts = [slice(i * tile, (i + 1) * tile) for i in range(4)]
    moves = [
        pltpu.make_async_copy(weight.at[:, cut], kept.at[:, cut], came.at[i])
        for i, cut in enumerate(cuts)
    ]
    for move in moves:
        move.start()
    leave = mask_and_leave(recv, hand, value, partner, done)
    product = 0.0
    for move, cut in zip(moves, cuts):
        move.wait()
        product = product + product_of(value[:, cut], kept[:, cut])
    spread(product, True, mine, left, right)
    leave.wait()


def keep_kernel(weight, token, kept, done):
    move = pltpu.make_async_copy(weight, kept, done)
    move.start()
    move.wait()


def last_kernel(first, recv, hand, weight, scale, mine, left, right, partner, *rest):
    outs, value, done = rest[:-2], rest[-2], rest[-1]
    leave = mask_and_leave(recv, hand, value, partner, done)
    product = product_of(value[...], weight[...])
    theirs = jnp.concatenate([left[...], right[...]], axis=1)
    total = jnp.concatenate([mine[...], product], axis=0) + theirs.astype(F32)
    give(first, scale, total, *outs)
    leave.wait()


def weight_kernel(count, turned, *refs):
    partners, out = refs[:count], refs[-1]
    rhs = jnp.concatenate([p[...] for p in partners], axis=0)
    out[...] = jnp.dot(turned[...], rhs, preferred_element_type=F32)


def unpack(half, info, back):
    slot, block = info[0:1, :], info[1:2, :]
    chips, part, width = back.shape
    target = jnp.where(slot // part == half, block * part + slot % part, -1)
    hot = (iota((chips * part, target.shape[1]), 0) == target).astype(F32).astype(BF16)
    return lax.dot_general(
        hot,
        back[...].reshape(chips * part, width),
        (((0,), (0,)), ((), ())),
        preferred_element_type=F32,
    )


def unpack_kernel(info, back, left, right):
    rows = unpack(0, info, back).astype(BF16)
    half = left.shape[1]
    left[...] = rows[:, :half]
    right[...] = rows[:, half:]


def choose_kernel(left, right, out):
    is_up = lax.axis_index("section") == 0
    out[...] = jnp.where(is_up, left[...], right[...])


def final_kernel(info, back, left, right, out):
    is_up = lax.axis_index("section") == 0
    early = jnp.where(is_up, left[...], right[...]).astype(F32)
    out[...] = (unpack(1, info, back) + early).astype(BF16)


def on_device(section_rows, lang_ids, lang_table, lang_counts, temp_num, weights):
    is_up = lax.axis_index("section") == 0
    replicas = lax.axis_size("dp")
    chips = replicas // 2
    rows_dev = lang_ids.shape[0]
    cap = 2 * rows_dev // chips
    width = section_rows.shape[2]
    own_weight = weights[0]
    ff_dev = own_weight.shape[1]

    halves = 2
    part = cap // halves
    wide = width + NOTES

    *packed, info, fast_weight = call(
        place_kernel,
        (
            *(sds((chips, part, wide), BF16) for _ in range(halves)),
            sds((8, rows_dev), I32),
            pltpu.VMEM(own_weight.shape, BF16),
        ),
        *(
            pltpu.with_memory_space_constraint(value, pltpu.HBM)
            for value in (
                lang_ids.reshape(1, -1),
                lang_table.reshape(1, -1),
                lang_counts,
                section_rows[0],
                own_weight,
            )
        ),
        scratch=[
            pltpu.VMEM((1, rows_dev), I32),
            pltpu.VMEM((1, lang_table.shape[0]), I32),
            pltpu.VMEM(lang_counts.shape, I32),
            pltpu.VMEM((rows_dev, width), BF16),
            pltpu.SemaphoreType.DMA((5,)),
        ],
        spec=pl.BlockSpec(memory_space=pltpu.HBM),
    )

    hands, received, partners = [], [], []

    def product(inputs, pieces, sizes, at=0, sofar=()):
        return call(
            functools.partial(product_kernel, len(inputs), pieces, at),
            tuple(sds((size, ff_dev), BF16) for size in sizes),
            *inputs,
            fast_weight,
            *sofar,
            scratch=[pltpu.VMEM((sum(piece[3] for piece in pieces), width), BF16)],
            aliases={len(inputs) + 1: 0} if sofar else {},
        )

    came, chunks = [], []
    for p in range(halves):
        packed[p] = after(packed[p], *(hands[-1] if p else ()))
        own = same_core_exchange(packed[p])
        came += [own, sibling(own)]
        cores = (1, 0) if p else (0, 1)
        chunks.append([(c, 0, r, part) for c in cores for r in range(chips)])
        rows = 2 * part * chips
        if p:
            hand = product(came[2:], chunks[p], [5 * rows // 8, 3 * rows // 8])
        else:
            mine = product(came[:1], chunks[p][:chips], [rows])
            theirs = [(0, *rest) for _, *rest in chunks[p][chips:]]
            hand = product(came[1:], theirs, [rows], rows // 2, mine)
        hands.append(hand)
        received.append(across(hand))
    layout = [(2 * p + which, *rest) for p in range(halves) for which, *rest in chunks[p]]
    total_rows = halves * rows
    scale, turned = call(
        functools.partial(tail_kernel, layout, [0, 1]),
        (sds((total_rows, 1), F32), sds((width, total_rows), BF16)),
        after(temp_num.reshape(1, -1), *hands[-1]),
        *came,
        scratch=[pltpu.VMEM((total_rows, width), BF16)],
    )
    count = rows // 2
    half = sds((count, width // 2), BF16)
    late_rows = [hand.shape[0] for hand in hands[1]]

    def room(size):
        return [pltpu.VMEM((size, ff_dev), BF16), pltpu.SemaphoreType.DMA]

    def backed(kernel, size, outs, args, scratch=(), specs=VMEM):
        partner, *rest = call(
            kernel,
            (pltpu.HBM((size, ff_dev), BF16), *outs),
            *args,
            scratch=[*room(size), *scratch],
            out_spaces=(pltpu.HBM, *(pltpu.VMEM for _ in outs)),
            spec=specs,
        )
        partners.append(partner)
        return rest

    mine, left, right = backed(
        back_kernel,
        rows,
        [sds((count, width), F32), half, half],
        [after(received[0][0], scale, *hands[1]), hands[0][0], fast_weight],
    )
    stack = call(
        functools.partial(stack_kernel, 0),
        sds((chips, part, width), BF16),
        scale,
        mine,
        sibling(left),
        sibling(right),
    )
    early_left, early_right = call(
        unpack_kernel,
        (sds((rows_dev, width // 2), BF16),) * 2,
        info,
        same_core_exchange(stack),
    )
    far_weight = pltpu.with_memory_space_constraint(own_weight, pltpu.HBM)
    in_hbm = pl.BlockSpec(memory_space=pltpu.HBM)
    mine, left, right = backed(
        fetch_kernel,
        late_rows[0],
        [sds((late_rows[0] - count, width), F32), half, half],
        [after(received[1][0], partners[0], stack), hands[1][0], far_weight],
        scratch=[pltpu.VMEM(own_weight.shape, BF16), pltpu.SemaphoreType.DMA((4,))],
        specs=[VMEM, VMEM, in_hbm],
    )
    (kept,) = call(
        keep_kernel,
        (pltpu.VMEM(own_weight.shape, BF16),),
        far_weight,
        after(info, early_left, mine),
        scratch=[pltpu.SemaphoreType.DMA],
        spec=[in_hbm, VMEM],
    )
    late_left, late_right = backed(
        functools.partial(last_kernel, rows + count),
        late_rows[1],
        [sds((chips, part, width // 2), BF16)] * 2,
        [
            after(received[1][1], partners[1], kept),
            hands[1][1],
            kept,
            scale,
            mine,
            sibling(left),
            sibling(right),
        ],
    )
    (late_recv,) = across([late_right])
    tile = 512
    first_tiles = ff_dev // tile // 4

    def weight_part(start, steps, sofar=()):
        return pl.pallas_call(
            functools.partial(weight_kernel, len(partners)),
            out_shape=sds((width, ff_dev), F32),
            grid=(steps,),
            in_specs=[pl.BlockSpec((width, total_rows), lambda j: (0, 0))]
            + [pl.BlockSpec((p.shape[0], tile), lambda j: (0, start + j)) for p in partners]
            + [pl.BlockSpec(memory_space=pl.ANY) for _ in sofar],
            out_specs=pl.BlockSpec((width, tile), lambda j: (0, start + j)),
            input_output_aliases={1 + len(partners): 0} if sofar else {},
            compiler_params=pltpu.CompilerParams(vmem_limit_bytes=60 << 20),
            cost_estimate=pl.CostEstimate(
                flops=1000, bytes_accessed=1000, transcendentals=0
            ),
        )(turned, *partners, *sofar)

    weight_grad = weight_part(0, first_tiles)
    late_recv = after(late_recv, weight_grad)
    late = call(choose_kernel, sds((chips, part, width // 2), BF16), late_left, late_recv)
    late = same_core_exchange(late)
    (early_recv,) = across([after(early_right, late_recv)])
    weight_grad = weight_part(first_tiles, ff_dev // tile - first_tiles, [weight_grad])
    info = after(info, weight_grad)
    input_grad = pl.pallas_call(
        final_kernel,
        out_shape=sds((rows_dev, width // 2), BF16),
        compiler_params=pltpu.CompilerParams(vmem_limit_bytes=12 << 20),
        cost_estimate=pl.CostEstimate(flops=1000, bytes_accessed=1000, transcendentals=0),
    )(info, late, early_left, early_recv)
    return (weight_grad[None], input_grad)


def solution(mesh):
    return jax.shard_map(
        on_device,
        mesh=mesh,
        in_specs=(
            P("section", "dp", None),
            P("dp"),
            P(),
            P("dp", None),
            P(),
            P("section", None, "dp"),
        ),
        out_specs=(P("section", None, "dp"), P("dp", "section")),
        check_vma=False,
    )
```
